32 devices in a mesh: groups: 2 (over x), seq: 16 (over z, y, core).
Axes of the slice: x: 2, y: 2, z: 4, core: 2. Of those that a mesh axis runs over, the one named last changes fastest.
Arguments:
- frame_queries: bfloat16 [4096, 768], P(('groups', 'seq')), parts along dimension 0, may hold values from -8 to 8
- frame_keys: bfloat16 [4096, 768], P(('groups', 'seq')), parts along dimension 0, may hold values from -8 to 8
- frame_values: bfloat16 [4096, 768], P(('groups', 'seq')), parts along dimension 0, may hold values from -6 to 6
- cotangent: bfloat16 [4096, 768], P(('groups', 'seq')), parts along dimension 0, may hold values from -6 to 6
- frame_mask: int32 [4096], P(('groups', 'seq')), parts along dimension 0, may hold values from 0 to 1, as said below
- global_rows: int32 [256], P('groups'), parts along dimension 0, may hold values from 0 to 1023, as said below
- position_bias: float32 [12, 255], replicated, may hold values from -4 to 4
Outputs:
- attended: bfloat16 [4096, 768], P(('groups', 'seq')), parts along dimension 0
- grad_queries: bfloat16 [4096, 768], P(('groups', 'seq')), parts along dimension 0
- grad_keys: bfloat16 [4096, 768], P(('groups', 'seq')), parts along dimension 0
- grad_values: bfloat16 [4096, 768], P(('groups', 'seq')), parts along dimension 0
- grad_bias: float32 [24, 255], P('groups'), parts along dimension 0
The draws below stay inside these ranges and needn't reach their ends.
There are 2 independent parts, one for each index of `groups`. The reference program is written for one: setup_inputs(seed, part) draws one part's arguments, and reference() takes and returns one part's arrays. A program takes and returns all parts, laid end to end along the dimension named above; an argument that names none is the same for every part. Nothing has to cross between parts.
Inputs may be any that keep to these rules, and one draw needn't show every extreme that they name: `frame_mask`: ones on a prefix of more than 1024 frames and zeros after it; at least one zero. `global_rows`: 128 distinct frame indices below 1024, so all on live frames; 0 and 1023 both occur.
All inputs are finite; a program needn't handle non-finite values.
Results may differ from the reference program's by a relative error of at most 0.008.
The reference program's roundings to bfloat16 on the way count: a program that leaves them out, or rounds other values in their place, can miss the bound.
Values may be sent and summed in bfloat16 or wider, within the bound.
No kernel may reach another device: no remote copies, remote signals or barrier semaphores. Data moves between devices by JAX's collectives and lax.ppermute only.
A program may use at most 64 MiB of HBM per device.

```python
import jax
import jax.numpy as jnp
from jax import lax

HEADS = 12
HSIZE = 64
BLK = 64
GROWS = 128
FRAMES = 2048
ATT_WIDTH = 768


def memory_positions(key):
    half_frames = FRAMES // 2
    middle = jax.random.permutation(jax.random.fold_in(key, 11), half_frames - 2)[:GROWS - 2] + 1
    ends = jnp.array([0, half_frames - 1], dtype=jnp.int32)
    positions = jnp.concatenate([middle.astype(jnp.int32), ends])
    order = jax.random.permutation(jax.random.fold_in(key, 12), GROWS)
    return positions[order].astype(jnp.int32)


def draw_frame_queries(key, part):
    base = jnp.clip(jax.random.normal(jax.random.fold_in(key, 41), (FRAMES, HEADS, HSIZE), jnp.float32), -8.0, 8.0)
    return base.reshape(FRAMES, HEADS * HSIZE).astype(jnp.bfloat16)


def draw_frame_keys(key, part):
    base = jnp.clip(jax.random.normal(jax.random.fold_in(key, 51), (FRAMES, HEADS, HSIZE), jnp.float32), -8.0, 8.0)
    return base.reshape(FRAMES, HEADS * HSIZE).astype(jnp.bfloat16)


def draw_frame_mask(key, part):
    trimmed = jax.random.randint(jax.random.fold_in(key, 61), (), 1, FRAMES // 2)
    return (jnp.arange(FRAMES) < FRAMES - trimmed).astype(jnp.int32)


def draw_global_rows(key, part):
    return memory_positions(key)


def steps_of(stream_key, shape, pieces, smallest, high):
    def one(dim, parts):
        draws = jax.random.uniform(jax.random.fold_in(jax.random.fold_in(stream_key, 6), dim), (parts,), jnp.float32, smallest / len(pieces), high / len(pieces))
        return jnp.repeat(jnp.exp(draws), shape[dim] // parts).reshape((-1,) + (1,) * (len(shape) - dim - 1))

    factor_of = one(*pieces[0])
    for cut in pieces[1:]:
        factor_of = factor_of * one(*cut)
    return factor_of


def noise(key, shape, width, most, pieces=(), held_as=jnp.bfloat16):
    values = width * jax.random.normal(key, shape, jnp.float32)
    if pieces:
        values = values * steps_of(key, shape, pieces, -0.22, 0.18)
    return jnp.clip(values, -most, most).astype(held_as)


def setup_inputs(seed: int = 0, part: int = 0) -> dict:
    key_of = jax.random.split(jax.random.key(seed), 8)
    part_keys = jax.random.split(jax.random.fold_in(key_of[7], part), 8)
    return {
        "frame_queries": draw_frame_queries(jax.random.fold_in(jax.random.fold_in(key_of[7], part), 71), part),
        "frame_keys": draw_frame_keys(jax.random.fold_in(jax.random.fold_in(key_of[7], part), 71), part),
        "frame_values": noise(part_keys[2], (FRAMES, ATT_WIDTH), 1.0, 6.0, ((0, 16),)),
        "cotangent": noise(part_keys[3], (FRAMES, ATT_WIDTH), 1.0, 6.0, ((0, 16),)),
        "frame_mask": draw_frame_mask(jax.random.fold_in(jax.random.fold_in(key_of[7], part), 71), part),
        "global_rows": draw_global_rows(jax.random.fold_in(jax.random.fold_in(key_of[7], part), 71), part),
        "position_bias": noise(key_of[6], (HEADS, 4 * BLK - 1), 1.0, 4.0, (), jnp.float32),
    }


NEG_BIG = -1.0e30


def bias_table(position_bias):
    row_ids = jnp.arange(BLK)[:, None]
    col_ids = jnp.arange(3 * BLK)[None, :]
    return position_bias[:, col_ids - row_ids + BLK - 1]


def reference(frame_queries, frame_keys, frame_values, cotangent, frame_mask, global_rows, position_bias):
    att_width = HEADS * HSIZE
    factor = HSIZE ** -0.5
    blocks = FRAMES // BLK
    window = 3 * BLK
    live_rows = frame_mask == 1
    memory_query = frame_queries[global_rows].reshape(GROWS, HEADS, HSIZE)
    memory_key = frame_keys[global_rows].reshape(GROWS, HEADS, HSIZE)
    memory_value = frame_values[global_rows].reshape(GROWS, HEADS, HSIZE)
    memory_grad = cotangent[global_rows].reshape(GROWS, HEADS, HSIZE)
    key_pad = jnp.pad(frame_keys, ((BLK, BLK), (0, 0)))
    value_pad = jnp.pad(frame_values, ((BLK, BLK), (0, 0)))
    live_pad = jnp.pad(live_rows, (BLK, BLK))
    table = bias_table(position_bias)

    def band_probs(start):
        query_rows = lax.dynamic_slice_in_dim(frame_queries, start, BLK, 0).reshape(BLK, HEADS, HSIZE)
        key_win = lax.dynamic_slice_in_dim(key_pad, start, window, 0).reshape(window, HEADS, HSIZE)
        value_win = lax.dynamic_slice_in_dim(value_pad, start, window, 0).reshape(window, HEADS, HSIZE)
        usable = lax.dynamic_slice_in_dim(live_pad, start, window, 0)
        keys_all = jnp.concatenate([key_win, memory_key], axis=0)
        values_all = jnp.concatenate([value_win, memory_value], axis=0)
        scores = jnp.einsum("ihs,jhs->hij", query_rows.astype(jnp.float32), keys_all.astype(jnp.float32)) * factor
        band_part = jnp.where(usable[None, None, :], scores[..., :window] + table, NEG_BIG)
        scores = jnp.concatenate([band_part, scores[..., window:]], axis=2)
        row_top = jnp.max(scores, axis=2, keepdims=True)
        raised = jnp.exp(scores - row_top)
        band_probs_f = raised / jnp.sum(raised, axis=2, keepdims=True)
        return query_rows, keys_all, values_all, band_probs_f

    def band_forward(index):
        start = index.astype(jnp.int32) * BLK
        query_rows, keys_all, values_all, band_probs_f = band_probs(start)
        rounded = lax.optimization_barrier(band_probs_f.astype(jnp.bfloat16)).astype(jnp.float32)
        return jnp.einsum("hij,jhs->ihs", rounded, values_all.astype(jnp.float32)).astype(jnp.bfloat16)

    band_out = lax.map(band_forward, jnp.arange(blocks)).reshape(FRAMES, att_width)

    key_heads = frame_keys.reshape(FRAMES, HEADS, HSIZE).transpose(1, 0, 2)
    value_heads = frame_values.reshape(FRAMES, HEADS, HSIZE).transpose(1, 0, 2)

    def global_head(items):
        query_head, key_head, value_head, grad_head = items
        scores = jnp.dot(query_head, key_head.T, preferred_element_type=jnp.float32) * factor
        scores = jnp.where(live_rows[None, :], scores, NEG_BIG)
        row_top = jnp.max(scores, axis=1, keepdims=True)
        weights = jnp.where(live_rows[None, :], jnp.exp(scores - row_top), 0.0)
        total = jnp.sum(weights, axis=1, keepdims=True)
        numerator = jnp.dot(weights, value_head.astype(jnp.float32), precision=lax.Precision.HIGHEST)
        out_head = (numerator / total).astype(jnp.bfloat16)
        shares = weights / total
        grad_share = jnp.dot(grad_head, value_head.T, preferred_element_type=jnp.float32)
        row_dot = jnp.sum(grad_head.astype(jnp.float32) * out_head.astype(jnp.float32), axis=1, keepdims=True)
        grad_scores = lax.optimization_barrier((shares * (grad_share - row_dot)).astype(jnp.bfloat16))
        shares_low = lax.optimization_barrier(shares.astype(jnp.bfloat16))
        dq_head = factor * jnp.dot(grad_scores, key_head, preferred_element_type=jnp.float32)
        dk_head = factor * jnp.dot(grad_scores.T, query_head, preferred_element_type=jnp.float32)
        dv_head = jnp.dot(shares_low.T, grad_head, preferred_element_type=jnp.float32)
        return out_head, dq_head, dk_head, dv_head

    memory_out, dq_memory, dk_wide, dv_wide = lax.map(
        global_head,
        (memory_query.transpose(1, 0, 2), key_heads, value_heads, memory_grad.transpose(1, 0, 2)))
    memory_out = memory_out.transpose(1, 0, 2).reshape(GROWS, att_width)
    dq_memory = dq_memory.transpose(1, 0, 2).reshape(GROWS, att_width)
    dk_wide = dk_wide.transpose(1, 0, 2).reshape(FRAMES, att_width)
    dv_wide = dv_wide.transpose(1, 0, 2).reshape(FRAMES, att_width)

    attended = band_out.at[global_rows].set(memory_out)
    attended = jnp.where(live_rows[:, None], attended, jnp.zeros_like(attended))

    is_memory = jnp.zeros((FRAMES,), jnp.int32).at[global_rows].set(1) == 1
    keep_rows = live_rows & jnp.logical_not(is_memory)
    grad_in = jnp.where(keep_rows[:, None], cotangent, jnp.zeros_like(cotangent))

    def band_back(carry, index):
        bias_acc, key_acc, value_acc, mem_key_acc, mem_value_acc = carry
        start = index.astype(jnp.int32) * BLK
        query_rows, keys_all, values_all, band_probs_f = band_probs(start)
        grad_rows = lax.dynamic_slice_in_dim(grad_in, start, BLK, 0).reshape(BLK, HEADS, HSIZE).astype(jnp.float32)
        out_rows = lax.dynamic_slice_in_dim(band_out, start, BLK, 0).reshape(BLK, HEADS, HSIZE).astype(jnp.float32)
        grad_share = jnp.einsum("ihs,jhs->hij", grad_rows, values_all.astype(jnp.float32))
        row_dot = jnp.sum(grad_rows * out_rows, axis=2).T
        grad_scores = band_probs_f * (grad_share - row_dot[..., None])
        grad_low = lax.optimization_barrier(grad_scores.astype(jnp.bfloat16)).astype(jnp.float32)
        probs_low = lax.optimization_barrier(band_probs_f.astype(jnp.bfloat16)).astype(jnp.float32)
        dq_rows = factor * jnp.einsum("hij,jhs->ihs", grad_low, keys_all.astype(jnp.float32))
        dk_all = factor * jnp.einsum("hij,ihs->jhs", grad_low, query_rows.astype(jnp.float32))
        dv_all = jnp.einsum("hij,ihs->jhs", probs_low, grad_rows)
        old_keys = lax.dynamic_slice_in_dim(key_acc, start, window, 0)
        key_acc = lax.dynamic_update_slice_in_dim(key_acc, old_keys + dk_all[:window].reshape(window, att_width), start, 0)
        old_values = lax.dynamic_slice_in_dim(value_acc, start, window, 0)
        value_acc = lax.dynamic_update_slice_in_dim(value_acc, old_values + dv_all[:window].reshape(window, att_width), start, 0)
        new_carry = (bias_acc + grad_scores[..., :window], key_acc, value_acc,
                     mem_key_acc + dk_all[window:], mem_value_acc + dv_all[window:])
        return new_carry, dq_rows

    start_carry = (jnp.zeros((HEADS, BLK, window), jnp.float32),
                   jnp.zeros((FRAMES + 2 * BLK, att_width), jnp.float32),
                   jnp.zeros((FRAMES + 2 * BLK, att_width), jnp.float32),
                   jnp.zeros((GROWS, HEADS, HSIZE), jnp.float32),
                   jnp.zeros((GROWS, HEADS, HSIZE), jnp.float32))
    final_carry, dq_band = lax.scan(band_back, start_carry, jnp.arange(blocks))
    bias_acc, key_acc, value_acc, mem_key_acc, mem_value_acc = final_carry
    dq_band = dq_band.reshape(FRAMES, att_width)

    row_ids = jnp.arange(BLK)[:, None]
    col_ids = jnp.arange(window)[None, :]
    grad_bias = jnp.zeros((HEADS, 4 * BLK - 1), jnp.float32).at[:, col_ids - row_ids + BLK - 1].add(bias_acc)

    grad_queries = dq_band.at[global_rows].add(dq_memory).astype(jnp.bfloat16)
    grad_keys = (key_acc[BLK:-BLK] + dk_wide).at[global_rows].add(mem_key_acc.reshape(GROWS, att_width)).astype(jnp.bfloat16)
    grad_values = (value_acc[BLK:-BLK] + dv_wide).at[global_rows].add(mem_value_acc.reshape(GROWS, att_width)).astype(jnp.bfloat16)
    return attended, grad_queries, grad_keys, grad_values, grad_bias
```

```python
import jax
import jax.numpy as jnp
from jax import lax
from jax.experimental import pallas as pl
from jax.experimental.pallas import tpu as pltpu
from jax.sharding import PartitionSpec as P

NEG_BIG = -1e30
DEAD = 64.0
BIAS_ROWS = 8
BF16 = jnp.bfloat16
F32 = jnp.float32


def mm(a, b):
    return jnp.dot(a, b, preferred_element_type=F32)


def split2(x):
    high = x.astype(BF16)
    return high, (x - high.astype(F32)).astype(BF16)


def iota(shape, dim):
    return lax.broadcasted_iota(jnp.int32, shape, dim)


def swap_halves(x):
    half = x.shape[1] // 2
    return jnp.concatenate([x[:, half:], x[:, :half]], axis=1)


def pack_kernel(mask_ref, q_ref, k_ref, v_ref, g_ref, out_ref):
    slots, rows, _ = out_ref.shape
    pairs = q_ref.shape[1] // 128
    live = jnp.sum(mask_ref[...])
    alive = iota((rows, 128), 0) < live
    low = iota((rows, 128), 1) < 64
    for i in range(pairs):
        at = slice(128 * i, 128 * (i + 1))
        q, k, v = q_ref[:, at], k_ref[:, at], v_ref[:, at]
        g = jnp.where(alive, g_ref[:, at], jnp.asarray(DEAD, BF16))
        out_ref[2 * i, :, 0:128] = jnp.where(low, k, swap_halves(v))
        out_ref[2 * i + 1, :, 0:128] = jnp.where(low, swap_halves(k), v)
        out_ref[2 * i, :, 128:256] = jnp.where(low, q, swap_halves(g))
        out_ref[2 * i + 1, :, 128:256] = jnp.where(low, swap_halves(q), g)

    @pl.loop(2 * pairs, slots)
    def _(s):
        out_ref[s] = jnp.zeros(out_ref.shape[1:], BF16)


def unpack_kernel(in_ref, att_ref, dq_ref, dk_ref, dv_ref, gb_ref):
    rows = att_ref.shape[0]
    pairs = att_ref.shape[1] // 128
    low = iota((rows, 128), 1) < 64
    for i in range(pairs):
        at = slice(128 * i, 128 * (i + 1))
        a, b = in_ref[2 * i, :rows, 0:128], in_ref[2 * i + 1, :rows, 0:128]
        dk_ref[:, at] = jnp.where(low, a, swap_halves(b))
        dv_ref[:, at] = jnp.where(low, swap_halves(a), b)
        a, b = in_ref[2 * i, :rows, 128:256], in_ref[2 * i + 1, :rows, 128:256]
        dq_ref[:, at] = jnp.where(low, a, swap_halves(b))
        att_ref[:, at] = jnp.where(low, swap_halves(a), b)
    for h in range(2 * pairs):
        parts = in_ref[h, rows:, :].astype(F32)
        whole = parts[0:1] + parts[1:2] + parts[2:3]
        gb_ref[h : h + 1, :] = whole[:, : gb_ref.shape[1]]


def shear(x, first, step):
    rows, lanes = x.shape
    row = iota(x.shape, 0)
    x = pltpu.roll(x, first % lanes, 1)
    bit = 1
    while bit < rows:
        x = jnp.where((row & bit) != 0, pltpu.roll(x, (step * bit) % lanes, 1), x)
        bit *= 2
    return x


def core_kernel(
    rows_ref, bias_ref, x_ref, y_ref, kv_ref, kvt_ref, qd_ref, qdt_ref, ww_ref, tb_ref, gb_ref, gm_ref
):
    slots, tile, _ = x_ref.shape
    frames = slots * tile
    blk = tile // 2
    heads, span = bias_ref.shape
    memory = rows_ref.shape[1]
    scale = 64 ** (-0.5)
    owner = lax.axis_index("seq")

    @pl.when(owner < heads)
    def _():
        low_lane = iota((tile, 128), 1) < 64
        low_row = iota((128, 128), 0) < 64
        gr_row = jnp.broadcast_to(rows_ref[...], (128, memory))
        gr_col = gr_row.T
        lane = iota((128, 128), 1)
        sub = iota((128, 128), 0)

        def count(s, c):
            g = x_ref[s, :, 128:256].astype(F32)
            return c + jnp.sum((g < 0.5 * DEAD).astype(F32), axis=0, keepdims=True)

        counts = lax.fori_loop(0, slots, count, jnp.zeros((1, 128), F32))
        length = jnp.max(counts[:, 64:65], axis=1, keepdims=True).astype(jnp.int32)

        def gather(s, c):
            pick = (gr_col == lane + s * tile).astype(BF16)
            return c + mm(pick, x_ref[s])

        mem = lax.fori_loop(0, slots // 2, gather, jnp.zeros((128, 256), F32))
        mkv = mem[:, 0:128].astype(BF16)
        mqo = jnp.where(lane < 64, mem[:, 128:256] * scale, mem[:, 128:256]).astype(BF16)
        mkv_t = mkv.T
        mqo_t = mqo.T

        zeros = jnp.zeros((blk, 128), BF16)
        kv_ref[0:blk, :] = zeros
        kv_ref[frames + blk :, :] = zeros
        ww_ref[0:blk, 0:128] = zeros.astype(F32)
        ww_ref[frames + blk :, 0:128] = zeros.astype(F32)

        def prepare(s, c):
            at = pl.multiple_of(s * tile, tile)
            kv_ref[pl.ds(pl.multiple_of(at + blk, blk), tile), :] = x_ref[s, :, 0:128]
            mine = jnp.max((gr_row == sub + at).astype(F32), axis=1, keepdims=True)
            keep = (mine < 0.5) & (sub[:, 0:1] + at < length)
            qd = x_ref[s, :, 128:256].astype(F32)
            qd = jnp.where(low_lane, qd * scale, jnp.where(keep, qd, 0.0)).astype(BF16)
            qd_ref[pl.ds(at, tile), :] = qd
            qdt_ref[:, pl.ds(at, tile)] = qd.T
            return c

        lax.fori_loop(0, slots, prepare, 0)

        def turn(s, c):
            at = pl.multiple_of(s * tile, tile)
            kvt_ref[:, pl.ds(at, tile)] = kv_ref[pl.ds(at, tile), :].T
            return c

        lax.fori_loop(0, slots + 1, turn, 0)

        head = jnp.minimum(owner, heads - 1)
        b_row = jnp.concatenate([bias_ref[pl.ds(head, 1), :], jnp.zeros((1, 384 - span), F32)], axis=1)
        table = shear(jnp.broadcast_to(b_row, (128, 384)), 1 - blk, 1)[:, : 2 * tile].T
        gap = iota(table.shape, 0) // blk - iota(table.shape, 1) // blk
        tb_ref[...] = jnp.where((gap >= 0) & (gap <= 2), table, NEG_BIG)
        gb_ref[...] = jnp.zeros_like(gb_ref)
        gm_ref[...] = jnp.zeros_like(gm_ref)

        zero_t = jnp.zeros_like(mqo_t)
        wide_rhs = jnp.concatenate(
            [jnp.where(low_row, mqo_t, zero_t), jnp.where(low_row, zero_t, mqo_t)], axis=1
        )
        wide_back = jnp.concatenate(
            [jnp.where(low_lane, mqo, zero_t), jnp.where(low_lane, zero_t, mqo)], axis=0
        )

        def wide_scores(s, top):
            at = pl.multiple_of(s * tile + blk, blk)
            both = mm(kv_ref[pl.ds(at, tile), :], wide_rhs)
            w = jnp.where(sub + s * tile < length, both[:, 0:128], NEG_BIG)
            ww_ref[pl.ds(at, tile), 0:128] = w
            ww_ref[pl.ds(at, tile), 128:256] = both[:, 128:256]
            return jnp.maximum(top, jnp.max(w, axis=0, keepdims=True))

        top = lax.fori_loop(0, slots, wide_scores, jnp.full((1, 128), NEG_BIG, F32))

        def wide_sums(s, c):
            total, numer = c
            at = pl.multiple_of(s * tile + blk, blk)
            e = jnp.exp(ww_ref[pl.ds(at, tile), 0:128] - top)
            e = jnp.where(sub + s * tile < length, e, 0.0)
            ww_ref[pl.ds(at, tile), 0:128] = e
            v_t = x_ref[s, :, 0:128].T[64:128, :]
            high, rest = split2(e)
            numer = numer + mm(v_t, jnp.concatenate([high, rest], axis=1))
            return total + jnp.sum(e, axis=0, keepdims=True), numer

        total, numer = lax.fori_loop(
            0, slots, wide_sums, (jnp.zeros((1, 128), F32), jnp.zeros((64, 256), F32))
        )
        mem_out = ((numer[:, 0:128] + numer[:, 128:256]) / total).astype(BF16)
        mem_dot = jnp.sum(mqo_t[64:128].astype(F32) * mem_out.astype(F32), axis=0, keepdims=True)
        share = 1.0 / total

        def wide_grads(s, dq):
            at = pl.multiple_of(s * tile + blk, blk)
            p = ww_ref[pl.ds(at, tile), 0:128] * share
            dw = (p * (ww_ref[pl.ds(at, tile), 128:256] - mem_dot)).astype(BF16)
            k_t = x_ref[s, :, 0:128].T[0:64, :]
            ww_ref[pl.ds(at, tile), 0:128] = mm(
                jnp.concatenate([dw, p.astype(BF16)], axis=1), wide_back
            )
            return dq + mm(k_t, dw)

        mem_dq = lax.fori_loop(0, slots, wide_grads, jnp.zeros((64, 128), F32)) * scale
        dq_high, dq_rest = split2(mem_dq)
        mem_rows = jnp.concatenate([dq_high, mem_out, dq_rest, jnp.zeros_like(mem_out)], axis=0)

        def band(s, c):
            at = pl.multiple_of(s * tile, tile)
            win = pl.ds(at, 2 * tile)
            qd, qd_t = qd_ref[pl.ds(at, tile), :], qdt_ref[:, pl.ds(at, tile)]
            rhs = jnp.concatenate(
                [jnp.where(low_row, qd_t, zero_t), jnp.where(low_row, zero_t, qd_t)], axis=1
            )
            back = jnp.concatenate(
                [jnp.where(low_lane, qd, zero_t), jnp.where(low_lane, zero_t, qd)], axis=0
            )
            near, far = mm(kv_ref[win, :], rhs), mm(mkv, rhs)
            place = iota((2 * tile, 128), 0) + (at - blk)
            s_near = jnp.where(
                (place >= 0) & (place < length), near[:, 0:128] + tb_ref[...], NEG_BIG
            )
            s_far = far[:, 0:128]
            high = jnp.maximum(
                jnp.max(s_near, axis=0, keepdims=True), jnp.max(s_far, axis=0, keepdims=True)
            )
            e_near, e_far = jnp.exp(s_near - high), jnp.exp(s_far - high)
            inv = 1.0 / (
                jnp.sum(e_near, axis=0, keepdims=True) + jnp.sum(e_far, axis=0, keepdims=True)
            )
            p_near, p_far = e_near * inv, e_far * inv
            pb_near, pb_far = p_near.astype(BF16), p_far.astype(BF16)
            out = mm(kvt_ref[64:128, win], pb_near) + mm(mkv_t[64:128], pb_far)
            out = out.astype(BF16).astype(F32)
            row_dot = jnp.sum(qd_t[64:128].astype(F32) * out, axis=0, keepdims=True)
            ds_near = p_near * (near[:, 128:256] - row_dot)
            ds_far = p_far * (far[:, 128:256] - row_dot)
            gb_ref[...] += ds_near
            db_near, db_far = ds_near.astype(BF16), ds_far.astype(BF16)
            dq = mm(kvt_ref[0:64, win], db_near) + mm(mkv_t[0:64], db_far)
            ww_ref[win, 0:128] += mm(jnp.concatenate([db_near, pb_near], axis=1), back)
            gm_ref[...] += mm(jnp.concatenate([db_far, pb_far], axis=1), back)
            pick = (gr_col == lane + at).astype(F32)
            mine = jnp.max(pick, axis=0, keepdims=True)
            placed = mm(mem_rows, pick.astype(BF16))
            live = lane[0:1] + at < length
            out = jnp.where(live, jnp.where(mine > 0.5, placed[64:128], out), 0.0)
            dq = dq * scale + (placed[0:64] + placed[128:192])
            y_ref[s, 0:tile, 128:256] = jnp.concatenate([dq, out], axis=0).astype(BF16).T
            return c

        lax.fori_loop(0, slots, band, 0)

        mem_back = jnp.concatenate(split2(gm_ref[...]), axis=0)

        wide_bias = jnp.concatenate([gb_ref[...], jnp.zeros((128, 128), F32)], axis=0).T
        bias_sum = jnp.sum(shear(wide_bias, blk - 1, -1), axis=0, keepdims=True)[:, 0:256]
        b0 = bias_sum.astype(BF16).astype(F32)
        b1 = (bias_sum - b0).astype(BF16).astype(F32)
        b2 = bias_sum - b0 - b1
        bias_rows = jnp.concatenate(
            [b0, b1, b2, jnp.zeros((BIAS_ROWS - 3, 256), F32)], axis=0
        ).astype(BF16)

        def finish(s, c):
            at = pl.multiple_of(s * tile, tile)
            pick = (gr_row == sub + at).astype(BF16)
            grads = ww_ref[pl.ds(pl.multiple_of(at + blk, blk), tile), 0:128] + mm(
                jnp.concatenate([pick, pick], axis=1), mem_back
            )
            y_ref[s, 0:tile, 0:128] = grads.astype(BF16)
            y_ref[s, tile:, :] = bias_rows
            return c

        lax.fori_loop(0, slots, finish, 0)


def vmem(shape, dtype):
    return pltpu.VMEM(shape, dtype)


def local(
    frame_queries, frame_keys, frame_values, cotangent, frame_mask, global_rows, position_bias
):
    slots = lax.axis_size("seq")
    tile, width = frame_queries.shape
    heads, span = position_bias.shape
    memory = global_rows.shape[0]
    frames = slots * tile
    wide = pltpu.CompilerParams(vmem_limit_bytes=60 * 1024 * 1024)

    packed = pl.pallas_call(
        pack_kernel,
        out_shape=jax.ShapeDtypeStruct((slots, tile, 256), BF16),
        compiler_params=wide,
    )(frame_mask.reshape(1, tile), frame_queries, frame_keys, frame_values, cotangent)
    by_head = lax.all_to_all(packed, "seq", 0, 0, tiled=True)
    grads = pl.pallas_call(
        core_kernel,
        out_shape=jax.ShapeDtypeStruct((slots, tile + BIAS_ROWS, 256), BF16),
        scratch_shapes=[
            vmem((frames + tile, 128), BF16),
            vmem((128, frames + tile), BF16),
            vmem((frames, 128), BF16),
            vmem((128, frames), BF16),
            vmem((frames + tile, 256), F32),
            vmem((2 * tile, 128), F32),
            vmem((2 * tile, 128), F32),
            vmem((128, 128), F32),
        ],
        compiler_params=wide,
    )(global_rows.reshape(1, memory), position_bias, by_head)
    by_frame = lax.all_to_all(grads, "seq", 0, 0, tiled=True)
    rows = jax.ShapeDtypeStruct((tile, width), BF16)
    attended, dq, dk, dv, grad_bias = pl.pallas_call(
        unpack_kernel,
        out_shape=(rows, rows, rows, rows, jax.ShapeDtypeStruct((heads, span), F32)),
        compiler_params=wide,
    )(by_frame)
    return (attended, dq, dk, dv, grad_bias)


def solution(mesh):
    return jax.shard_map(
        local,
        mesh=mesh,
        in_specs=(
            P(("groups", "seq"), None),
            P(("groups", "seq"), None),
            P(("groups", "seq"), None),
            P(("groups", "seq"), None),
            P(("groups", "seq")),
            P("groups"),
            P(),
        ),
        out_specs=(
            P(("groups", "seq"), None),
            P(("groups", "seq"), None),
            P(("groups", "seq"), None),
            P(("groups", "seq"), None),
            P("groups", None),
        ),
        check_vma=False,
    )
```

```python
import jax
import jax.numpy as jnp
from jax import lax
from jax.experimental import pallas as pl
from jax.experimental.pallas import tpu as pltpu
from jax.sharding import PartitionSpec as P

NEG_BIG = -1e30
DEAD = 64.0
BIAS_ROWS = 8
GROUP = 8
BAND_GROUP = 16
BF16 = jnp.bfloat16
F32 = jnp.float32


def mm(a, b):
    return jnp.dot(a, b, preferred_element_type=F32)


def split2(x):
    high = x.astype(BF16)
    return high, (x - high.astype(F32)).astype(BF16)


def iota(shape, dim):
    return lax.broadcasted_iota(jnp.int32, shape, dim)


def swap_halves(x):
    half = x.shape[1] // 2
    return jnp.concatenate([x[:, half:], x[:, :half]], axis=1)


def pack_kernel(*refs):
    sources, out_ref, held, sem = refs[:5], refs[5], refs[6:11], refs[11]
    copies = [
        pltpu.make_async_copy(source, here, sem.at[i])
        for i, (source, here) in enumerate(zip(sources, held))
    ]
    for copy in copies:
        copy.start()
    mask_ref, k_ref, v_ref, q_ref, g_ref = held
    slots, rows, _ = out_ref.shape
    pairs = q_ref.shape[1] // 128
    low = iota((rows, 128), 1) < 64

    @pl.loop(2 * pairs, slots)
    def _(s):
        out_ref[s] = jnp.zeros(out_ref.shape[1:], BF16)

    for copy in copies[:3]:
        copy.wait()
    for i in range(pairs):
        at = slice(128 * i, 128 * (i + 1))
        k, v = k_ref[:, at], v_ref[:, at]
        out_ref[2 * i, :, 0:128] = jnp.where(low, k, swap_halves(v))
        out_ref[2 * i + 1, :, 0:128] = jnp.where(low, swap_halves(k), v)
    for copy in copies[3:]:
        copy.wait()
    alive = iota((rows, 128), 0) < jnp.sum(mask_ref[...])
    for i in range(pairs):
        at = slice(128 * i, 128 * (i + 1))
        q, g = q_ref[:, at], jnp.where(alive, g_ref[:, at], jnp.asarray(DEAD, BF16))
        out_ref[2 * i, :, 128:256] = jnp.where(low, q, swap_halves(g))
        out_ref[2 * i + 1, :, 128:256] = jnp.where(low, swap_halves(q), g)


def unpack_kernel(in_ref, att_ref, dq_ref, dk_ref, dv_ref, gb_ref):
    rows = att_ref.shape[0]
    pairs = att_ref.shape[1] // 128
    low = iota((rows, 128), 1) < 64
    for i in range(pairs):
        at = slice(128 * i, 128 * (i + 1))
        a, b = in_ref[2 * i, :rows, 0:128], in_ref[2 * i + 1, :rows, 0:128]
        dk_ref[:, at] = jnp.where(low, a, swap_halves(b))
        dv_ref[:, at] = jnp.where(low, swap_halves(a), b)
        a, b = in_ref[2 * i, :rows, 128:256], in_ref[2 * i + 1, :rows, 128:256]
        dq_ref[:, at] = jnp.where(low, a, swap_halves(b))
        att_ref[:, at] = jnp.where(low, swap_halves(a), b)
    for h in range(2 * pairs):
        parts = in_ref[h, rows:, :].astype(F32)
        whole = parts[0:1] + parts[1:2] + parts[2:3]
        gb_ref[h : h + 1, :] = whole[:, : gb_ref.shape[1]]


def shear(x, first, step):
    rows, lanes = x.shape
    row = iota(x.shape, 0)
    x = pltpu.roll(x, first % lanes, 1)
    bit = 1
    while bit < rows:
        x = jnp.where((row & bit) != 0, pltpu.roll(x, (step * bit) % lanes, 1), x)
        bit *= 2
    return x


def core_kernel(
    rows_ref, bias_ref, x_ref, y_ref, kv_ref, kvt_ref, qd_ref, qdt_ref, ww_ref, tb_ref, gb_ref, gm_ref
):
    slots, tile, _ = x_ref.shape
    frames = slots * tile
    blk = tile // 2
    heads, span = bias_ref.shape
    memory = rows_ref.shape[1]
    scale = 64 ** (-0.5)
    owner = lax.axis_index("seq")
    chunk = GROUP * tile

    @pl.when(owner < heads)
    def _():
        lane = iota((128, 128), 1)
        sub = iota((128, 128), 0)
        low_lane = lane < 64
        low_row = sub < 64
        gr_row = jnp.broadcast_to(rows_ref[...], (128, memory))
        gr_col = gr_row.T
        zero_t = jnp.zeros((128, 128), BF16)

        def side(top, bottom):
            return jnp.concatenate([top, bottom], axis=1)

        def spread(x_t):
            return side(jnp.where(low_row, x_t, zero_t), jnp.where(low_row, zero_t, x_t))

        def stack(x):
            return jnp.concatenate(
                [jnp.where(low_lane, x, zero_t), jnp.where(low_lane, zero_t, x)], axis=0
            )

        def over_rows(body, carry):
            carry = lax.fori_loop(
                0, slots // GROUP, lambda i, c: body(pl.multiple_of(i * chunk, chunk), chunk, c), carry
            )
            return body(frames, tile, carry)

        def usable(at, rows, length):
            place = iota((rows, 128), 0) + (at - blk)
            return (place >= 0) & (place < length)

        zeros = jnp.zeros((blk, 128), BF16)
        kv_ref[0:blk, :] = zeros
        kv_ref[frames + blk :, :] = zeros
        wide_low = iota((chunk, 128), 1) < 64
        wide_sub = iota((chunk, 128), 0)
        wide_lane = iota((128, chunk), 1)
        wide_row = jnp.broadcast_to(gr_row[0:1], (chunk, memory))
        wide_col = jnp.concatenate([gr_col] * GROUP, axis=1)
        ones = jnp.ones((memory, 128), BF16)

        def prepare(first_half):
            def body(i, c):
                count, mem = c
                at = pl.multiple_of(i * chunk, chunk)
                x = x_ref[pl.ds(i * GROUP, GROUP)].reshape(chunk, 256)
                kv_ref[pl.ds(pl.multiple_of(at + blk, blk), chunk), :] = x[:, 0:128]
                qd = x[:, 128:256].astype(F32)
                alive = qd < 0.5 * DEAD
                count = count + jnp.sum(alive.astype(F32), axis=0, keepdims=True)
                keep = alive
                if first_half:
                    mem = mem + mm((wide_col == wide_lane + at).astype(BF16), x)
                    mine = mm((wide_row == wide_sub + at).astype(BF16), ones)
                    keep = alive & (mine < 0.5)
                qd = jnp.where(wide_low, qd * scale, jnp.where(keep, qd, 0.0)).astype(BF16)
                qd_ref[pl.ds(at, chunk), :] = qd
                qdt_ref[:, pl.ds(at, chunk)] = qd.T
                return count, mem

            return body

        steps = slots // GROUP
        carry = (jnp.zeros((1, 128), F32), jnp.zeros((128, 256), F32))
        carry = lax.fori_loop(0, steps // 2, prepare(True), carry)
        count, mem = lax.fori_loop(steps // 2, steps, prepare(False), carry)
        length = jnp.max(count[:, 64:65], axis=1, keepdims=True).astype(jnp.int32)
        mkv = mem[:, 0:128].astype(BF16)
        mqo = jnp.where(low_lane, mem[:, 128:256] * scale, mem[:, 128:256]).astype(BF16)
        mkv_t = mkv.T
        mqo_t = mqo.T

        head = jnp.minimum(owner, heads - 1)
        b_row = side(bias_ref[pl.ds(head, 1), :], jnp.zeros((1, 384 - span), F32))
        table = shear(jnp.broadcast_to(b_row, (128, 384)), 1 - blk, 1)[:, : 2 * tile].T
        gap = iota(table.shape, 0) // blk - iota(table.shape, 1) // blk
        tb_ref[...] = jnp.where((gap >= 0) & (gap <= 2), table, NEG_BIG)
        gb_ref[...] = jnp.zeros_like(gb_ref)
        gm_ref[...] = jnp.zeros_like(gm_ref)

        wide_rhs = spread(mqo_t)
        wide_back = stack(mqo)

        def wide_scores(at, rows, top):
            kv = kv_ref[pl.ds(at, rows), :]
            kvt_ref[:, pl.ds(at, rows)] = kv.T
            both = mm(kv, wide_rhs)
            w = jnp.where(usable(at, rows, length), both[:, 0:128], NEG_BIG)
            ww_ref[pl.ds(at, rows), 0:128] = w
            ww_ref[pl.ds(at, rows), 128:256] = both[:, 128:256]
            return jnp.maximum(top, jnp.max(w, axis=0, keepdims=True))

        top = over_rows(wide_scores, jnp.full((1, 128), NEG_BIG, F32))

        def wide_sums(at, rows, c):
            total, numer = c
            e = jnp.exp(ww_ref[pl.ds(at, rows), 0:128] - top)
            e = jnp.where(usable(at, rows, length), e, 0.0)
            ww_ref[pl.ds(at, rows), 0:128] = e
            high, rest = split2(e)
            numer = numer + mm(kvt_ref[64:128, pl.ds(at, rows)], side(high, rest))
            return total + jnp.sum(e, axis=0, keepdims=True), numer

        total, numer = over_rows(wide_sums, (jnp.zeros((1, 128), F32), jnp.zeros((64, 256), F32)))
        mem_out = ((numer[:, 0:128] + numer[:, 128:256]) / total).astype(BF16)
        mem_dot = jnp.sum(mqo_t[64:128].astype(F32) * mem_out.astype(F32), axis=0, keepdims=True)
        share = 1.0 / total

        def wide_grads(at, rows, dq):
            p = ww_ref[pl.ds(at, rows), 0:128] * share
            dw = (p * (ww_ref[pl.ds(at, rows), 128:256] - mem_dot)).astype(BF16)
            ww_ref[pl.ds(at, rows), 0:128] = mm(side(dw, p.astype(BF16)), wide_back)
            return dq + mm(kvt_ref[0:64, pl.ds(at, rows)], dw)

        mem_dq = over_rows(wide_grads, jnp.zeros((64, 128), F32)) * scale
        dq_high, dq_rest = split2(mem_dq)
        mem_rows = jnp.concatenate([dq_high, mem_out, dq_rest], axis=0)

        def band(i, c):
            many = range(BAND_GROUP)
            slot = [i * BAND_GROUP + u for u in many]
            at = [pl.multiple_of(s * tile, tile) for s in slot]
            win = [pl.ds(a, 2 * tile) for a in at]
            qd = [qd_ref[pl.ds(a, tile), :] for a in at]
            qd_t = [qdt_ref[:, pl.ds(a, tile)] for a in at]
            rhs = [spread(x) for x in qd_t]
            near = [mm(kv_ref[win[u], :], rhs[u]) for u in many]
            far = [mm(mkv, rhs[u]) for u in many]
            p_near, p_far, pb_near, pb_far = [], [], [], []
            for u in many:
                s_near = jnp.where(
                    usable(at[u], 2 * tile, length), near[u][:, 0:128] + tb_ref[...], NEG_BIG
                )
                s_far = far[u][:, 0:128]
                high = jnp.maximum(
                    jnp.max(s_near, axis=0, keepdims=True), jnp.max(s_far, axis=0, keepdims=True)
                )
                e_near, e_far = jnp.exp(s_near - high), jnp.exp(s_far - high)
                inv = 1.0 / (
                    jnp.sum(e_near, axis=0, keepdims=True) + jnp.sum(e_far, axis=0, keepdims=True)
                )
                p_near.append(e_near * inv)
                p_far.append(e_far * inv)
                pb_near.append(p_near[u].astype(BF16))
                pb_far.append(p_far[u].astype(BF16))
            out = [
                mm(kvt_ref[64:128, win[u]], pb_near[u]) + mm(mkv_t[64:128], pb_far[u]) for u in many
            ]
            back = [stack(x) for x in qd]
            ds_near, db_near, db_far = [], [], []
            for u in many:
                out[u] = out[u].astype(BF16).astype(F32)
                row_dot = jnp.sum(qd_t[u][64:128].astype(F32) * out[u], axis=0, keepdims=True)
                ds_near.append(p_near[u] * (near[u][:, 128:256] - row_dot))
                db_near.append(ds_near[u].astype(BF16))
                db_far.append((p_far[u] * (far[u][:, 128:256] - row_dot)).astype(BF16))
            gb_ref[...] += sum(ds_near)
            dq = [mm(kvt_ref[0:64, win[u]], db_near[u]) + mm(mkv_t[0:64], db_far[u]) for u in many]
            d_near = [mm(side(db_near[u], pb_near[u]), back[u]) for u in many]
            d_far = [mm(side(db_far[u], pb_far[u]), back[u]) for u in many]
            gm_ref[...] += sum(d_far)
            parts = [d_near[0][0:tile]]
            for u in many[1:]:
                parts.append(d_near[u - 1][tile:] + d_near[u][0:tile])
            parts.append(d_near[-1][tile:])
            ww_ref[pl.ds(at[0], tile * (BAND_GROUP + 1)), 0:128] += jnp.concatenate(parts, axis=0)
            for u in many:
                pick = (gr_col == lane + at[u]).astype(F32)
                mine = jnp.max(pick, axis=0, keepdims=True)
                placed = mm(mem_rows, pick.astype(BF16))
                live = lane[0:1] + at[u] < length
                o = jnp.where(live, jnp.where(mine > 0.5, placed[64:128], out[u]), 0.0)
                d = dq[u] * scale + (placed[0:64] + placed[128:192])
                y_ref[slot[u], 0:tile, 128:256] = jnp.concatenate([d, o], axis=0).astype(BF16).T
            return c

        lax.fori_loop(0, slots // BAND_GROUP, band, 0)

        wide_bias = jnp.concatenate([gb_ref[...], jnp.zeros((128, 128), F32)], axis=0).T
        bias_sum = jnp.sum(shear(wide_bias, blk - 1, -1), axis=0, keepdims=True)[:, 0:256]
        b0 = bias_sum.astype(BF16).astype(F32)
        b1 = (bias_sum - b0).astype(BF16).astype(F32)
        b2 = bias_sum - b0 - b1
        bias_rows = jnp.concatenate(
            [b0, b1, b2, jnp.zeros((BIAS_ROWS - 3, 256), F32)], axis=0
        ).astype(BF16)

        mem_back = jnp.concatenate(split2(gm_ref[...]), axis=0)

        def finish(first_half):
            def body(i, c):
                at = pl.multiple_of(i * chunk, chunk)
                grads = ww_ref[pl.ds(pl.multiple_of(at + blk, blk), chunk), 0:128]
                if first_half:
                    pick = (wide_row == wide_sub + at).astype(BF16)
                    grads = grads + mm(side(pick, pick), mem_back)
                y_ref[pl.ds(i * GROUP, GROUP), 0:tile, 0:128] = grads.astype(BF16).reshape(
                    GROUP, tile, 128
                )
                for u in range(GROUP):
                    y_ref[i * GROUP + u, tile:, :] = bias_rows
                return c

            return body

        lax.fori_loop(0, steps // 2, finish(True), 0)
        lax.fori_loop(steps // 2, steps, finish(False), 0)


def vmem(shape, dtype):
    return pltpu.VMEM(shape, dtype)


def grant(frames):
    return pltpu.CompilerParams(vmem_limit_bytes=min(16 * frames // 2048, 60) * 1024 * 1024)


def core_call(by_head, rows, position_bias):
    slots, tile, _ = by_head.shape
    frames = slots * tile
    return pl.pallas_call(
        core_kernel,
        out_shape=jax.ShapeDtypeStruct((slots, tile + BIAS_ROWS, 256), BF16),
        scratch_shapes=[
            vmem((frames + tile, 128), BF16),
            vmem((128, frames + tile), BF16),
            vmem((frames, 128), BF16),
            vmem((128, frames), BF16),
            vmem((frames + tile, 256), F32),
            vmem((2 * tile, 128), F32),
            vmem((2 * tile, 128), F32),
            vmem((128, 128), F32),
        ],
        compiler_params=grant(frames),
    )(rows, position_bias, by_head)


def local(
    frame_queries, frame_keys, frame_values, cotangent, frame_mask, global_rows, position_bias
):
    slots = lax.axis_size("seq")
    tile, width = frame_queries.shape
    heads, span = position_bias.shape
    memory = global_rows.shape[0]
    frames = slots * tile

    hbm = pl.BlockSpec(memory_space=pltpu.MemorySpace.HBM)
    whole = pltpu.VMEM((tile, width), BF16)
    packed = pl.pallas_call(
        pack_kernel,
        out_shape=jax.ShapeDtypeStruct((slots, tile, 256), BF16),
        in_specs=[hbm] * 5,
        scratch_shapes=[
            pltpu.VMEM((1, tile), jnp.int32),
            whole,
            whole,
            whole,
            whole,
            pltpu.SemaphoreType.DMA((5,)),
        ],
        compiler_params=grant(frames),
    )(
        *(
            pltpu.with_memory_space_constraint(x, pltpu.MemorySpace.HBM)
            for x in (
                frame_mask.reshape(1, tile),
                frame_keys,
                frame_values,
                frame_queries,
                cotangent,
            )
        )
    )
    by_head = lax.all_to_all(packed, "seq", 0, 0, tiled=True)
    grads = core_call(by_head, global_rows.reshape(1, memory), position_bias)
    by_frame = lax.all_to_all(grads, "seq", 0, 0, tiled=True)
    rows = jax.ShapeDtypeStruct((tile, width), BF16)
    attended, dq, dk, dv, grad_bias = pl.pallas_call(
        unpack_kernel,
        out_shape=(rows, rows, rows, rows, jax.ShapeDtypeStruct((heads, span), F32)),
        compiler_params=grant(frames),
    )(by_frame)
    return (attended, dq, dk, dv, grad_bias)


def solution(mesh):
    return jax.shard_map(
        local,
        mesh=mesh,
        in_specs=(
            P(("groups", "seq"), None),
            P(("groups", "seq"), None),
            P(("groups", "seq"), None),
            P(("groups", "seq"), None),
            P(("groups", "seq")),
            P("groups"),
            P(),
        ),
        out_specs=(
            P(("groups", "seq"), None),
            P(("groups", "seq"), None),
            P(("groups", "seq"), None),
            P(("groups", "seq"), None),
            P("groups", None),
        ),
        check_vma=False,
    )
```

```python
import functools

import jax
import jax.numpy as jnp
from jax import lax
from jax.experimental import pallas as pl
from jax.experimental.pallas import tpu as pltpu
from jax.sharding import PartitionSpec as P

NEG_BIG = -1e30
DEAD = 64.0
BIAS_ROWS = 8
GROUP = 8
BAND_GROUP = 16
SKEW = 2
BF16 = jnp.bfloat16
F32 = jnp.float32


def mm(a, b):
    return jnp.dot(a, b, preferred_element_type=F32)


def split2(x):
    high = x.astype(BF16)
    return high, (x - high.astype(F32)).astype(BF16)


def iota(shape, dim):
    return lax.broadcasted_iota(jnp.int32, shape, dim)


def swap_halves(x):
    half = x.shape[1] // 2
    return jnp.concatenate([x[:, half:], x[:, :half]], axis=1)


def pack_kernel(*refs):
    sources, out_ref, held, sem = refs[:5], refs[5], refs[6:11], refs[11]
    copies = [
        pltpu.make_async_copy(source, here, sem.at[i])
        for i, (source, here) in enumerate(zip(sources, held))
    ]
    for copy in copies:
        copy.start()
    mask_ref, k_ref, v_ref, q_ref, g_ref = held
    slots, rows, _ = out_ref.shape
    pairs = q_ref.shape[1] // 128
    low = iota((rows, 128), 1) < 64

    @pl.loop(2 * pairs, slots)
    def _(s):
        out_ref[s] = jnp.zeros(out_ref.shape[1:], BF16)

    for copy in copies[:3]:
        copy.wait()
    for i in range(pairs):
        at = slice(128 * i, 128 * (i + 1))
        k, v = k_ref[:, at], v_ref[:, at]
        out_ref[2 * i, :, 0:128] = jnp.where(low, k, swap_halves(v))
        out_ref[2 * i + 1, :, 0:128] = jnp.where(low, swap_halves(k), v)
    for copy in copies[3:]:
        copy.wait()
    alive = iota((rows, 128), 0) < jnp.sum(mask_ref[...])
    for i in range(pairs):
        at = slice(128 * i, 128 * (i + 1))
        q, g = q_ref[:, at], jnp.where(alive, g_ref[:, at], jnp.asarray(DEAD, BF16))
        out_ref[2 * i, :, 128:256] = jnp.where(low, q, swap_halves(g))
        out_ref[2 * i + 1, :, 128:256] = jnp.where(low, swap_halves(q), g)


def unpack_kernel(in_ref, att_ref, dq_ref, dk_ref, dv_ref, gb_ref):
    rows = att_ref.shape[0]
    pairs = att_ref.shape[1] // 128
    low = iota((rows, 128), 1) < 64
    for i in range(pairs):
        at = slice(128 * i, 128 * (i + 1))
        a, b = in_ref[2 * i, :rows, 0:128], in_ref[2 * i + 1, :rows, 0:128]
        dk_ref[:, at] = jnp.where(low, a, swap_halves(b))
        dv_ref[:, at] = jnp.where(low, swap_halves(a), b)
        a, b = in_ref[2 * i, :rows, 128:256], in_ref[2 * i + 1, :rows, 128:256]
        dq_ref[:, at] = jnp.where(low, a, swap_halves(b))
        att_ref[:, at] = jnp.where(low, swap_halves(a), b)
    for h in range(2 * pairs):
        parts = in_ref[h, rows:, :].astype(F32)
        whole = parts[0:1] + parts[1:2] + parts[2:3]
        gb_ref[h : h + 1, :] = whole[:, : gb_ref.shape[1]]


def repeat(first, last, body, carry):
    if last - first > 2:
        return lax.fori_loop(first, last, body, carry)
    for i in range(first, last):
        carry = body(i, carry)
    return carry


def aligned(x, size):
    return x if isinstance(x, int) else pl.multiple_of(x, size)


def shear(x, first, step):
    rows, lanes = x.shape
    row = iota(x.shape, 0)
    x = pltpu.roll(x, first % lanes, 1)
    bit = 1
    while bit < rows:
        x = jnp.where((row & bit) != 0, pltpu.roll(x, (step * bit) % lanes, 1), x)
        bit *= 2
    return x


def core_kernel(
    rows_ref, bias_ref, x_ref, y_ref, kv_ref, kvt_ref, qd_ref, qdt_ref, ww_ref, tb_ref, gb_ref, gm_ref, pick_ref
):
    slots, tile, _ = x_ref.shape
    frames = slots * tile
    blk = tile // 2
    heads, span = bias_ref.shape
    memory = rows_ref.shape[1]
    scale = 64 ** (-0.5)
    owner = lax.axis_index("seq")
    chunk = GROUP * tile
    steps = slots // GROUP

    @pl.when(owner < heads)
    def _():
        lane = iota((128, 128), 1)
        sub = iota((128, 128), 0)
        low_lane = lane < 64
        low_row = sub < 64
        gr_row = jnp.broadcast_to(rows_ref[...], (128, memory))
        gr_col = gr_row.T
        zero_t = jnp.zeros((128, 128), BF16)

        def side(top, bottom):
            return jnp.concatenate([top, bottom], axis=1)

        def spread(x_t):
            return side(jnp.where(low_row, x_t, zero_t), jnp.where(low_row, zero_t, x_t))

        def stack(x):
            return jnp.concatenate(
                [jnp.where(low_lane, x, zero_t), jnp.where(low_lane, zero_t, x)], axis=0
            )

        def over_rows(body, carry):
            carry = repeat(
                0, steps - 1, lambda i, c: body(aligned(i * chunk, chunk), chunk, c), carry
            )
            return body(frames - chunk, chunk + tile, carry)

        def usable(at, rows, length):
            place = iota((rows, 128), 0) + (at - blk)
            inside = place < length
            if isinstance(at, int) and at >= blk:
                return inside
            return (place >= 0) & inside

        zeros = jnp.zeros((blk, 128), BF16)
        kv_ref[0:blk, :] = zeros
        kv_ref[frames + blk :, :] = zeros
        wide_low = iota((chunk, 128), 1) < 64
        wide_sub = iota((chunk, 128), 0)
        wide_lane = iota((128, chunk), 1)
        wide_row = jnp.broadcast_to(gr_row[0:1], (chunk, memory))
        wide_col = jnp.concatenate([gr_col] * GROUP, axis=1)
        ones = jnp.ones((memory, 128), BF16)

        def prepare(first_half):
            def body(i, c):
                count, mem = c
                at = aligned(i * chunk, chunk)
                x = x_ref[pl.ds(i * GROUP, GROUP)].reshape(chunk, 256)
                kv_ref[pl.ds(aligned(at + blk, blk), chunk), :] = x[:, 0:128]
                qd = x[:, 128:256].astype(F32)
                alive = qd < 0.5 * DEAD
                count = count + jnp.sum(alive.astype(F32), axis=0, keepdims=True)
                keep = alive
                if first_half:
                    pick = (wide_col == wide_lane + at).astype(BF16)
                    pick_ref[:, pl.ds(at, chunk)] = pick
                    mem = mem + mm(pick, x)
                    mine = mm((wide_row == wide_sub + at).astype(BF16), ones)
                    keep = alive & (mine < 0.5)
                qd = jnp.where(wide_low, qd * scale, jnp.where(keep, qd, 0.0)).astype(BF16)
                qd_ref[pl.ds(at, chunk), :] = qd
                qdt_ref[:, pl.ds(at, chunk)] = qd.T
                return count, mem

            return body

        carry = (jnp.zeros((1, 128), F32), jnp.zeros((128, 256), F32))
        carry = repeat(0, steps // 2, prepare(True), carry)
        count, mem = repeat(steps // 2, steps, prepare(False), carry)
        length = jnp.max(count[:, 64:65], axis=1, keepdims=True).astype(jnp.int32)
        mkv = mem[:, 0:128].astype(BF16)
        mqo = jnp.where(low_lane, mem[:, 128:256] * scale, mem[:, 128:256]).astype(BF16)
        mkv_t = mkv.T
        mqo_t = mqo.T

        head = jnp.minimum(owner, heads - 1)
        b_row = side(bias_ref[pl.ds(head, 1), :], jnp.zeros((1, 384 - span), F32))
        table = shear(jnp.broadcast_to(b_row, (128, 384)), 1 - blk, 1)[:, : 2 * tile].T
        gap = iota(table.shape, 0) // blk - iota(table.shape, 1) // blk
        tb_ref[...] = jnp.where((gap >= 0) & (gap <= 2), table, NEG_BIG)
        gb_ref[...] = jnp.zeros_like(gb_ref)
        gm_ref[...] = jnp.zeros_like(gm_ref)

        wide_rhs = spread(mqo_t)
        wide_back = stack(mqo)

        def wide_scores(at, rows, top):
            kv = kv_ref[pl.ds(at, rows), :]
            kvt_ref[:, pl.ds(at, rows)] = kv.T
            both = mm(kv, wide_rhs)
            w = jnp.where(usable(at, rows, length), both[:, 0:128], NEG_BIG)
            ww_ref[pl.ds(at, rows), 0:128] = w
            ww_ref[pl.ds(at, rows), 128:256] = both[:, 128:256]
            return jnp.maximum(top, jnp.max(w, axis=0, keepdims=True))

        top = over_rows(wide_scores, jnp.full((1, 128), NEG_BIG, F32))

        def wide_sums(at, rows, c):
            total, numer = c
            e = jnp.exp(ww_ref[pl.ds(at, rows), 0:128] - top)
            ww_ref[pl.ds(at, rows), 0:128] = e
            high, rest = split2(e)
            numer = numer + mm(kvt_ref[64:128, pl.ds(at, rows)], side(high, rest))
            return total + jnp.sum(e, axis=0, keepdims=True), numer

        total, numer = over_rows(wide_sums, (jnp.zeros((1, 128), F32), jnp.zeros((64, 256), F32)))
        mem_out = ((numer[:, 0:128] + numer[:, 128:256]) / total).astype(BF16)
        mem_dot = jnp.sum(mqo_t[64:128].astype(F32) * mem_out.astype(F32), axis=0, keepdims=True)
        share = 1.0 / total

        def wide_grads(at, rows, dq):
            p = ww_ref[pl.ds(at, rows), 0:128] * share
            dw = (p * (ww_ref[pl.ds(at, rows), 128:256] - mem_dot)).astype(BF16)
            ww_ref[pl.ds(at, rows), 0:128] = mm(side(dw, p.astype(BF16)), wide_back)
            return dq + mm(kvt_ref[0:64, pl.ds(at, rows)], dw)

        mem_dq = over_rows(wide_grads, jnp.zeros((64, 128), F32)) * scale
        dq_high, dq_rest = split2(mem_dq)
        mem_rows = jnp.concatenate([dq_high, mem_out, dq_rest, jnp.ones((16, 128), BF16)], axis=0)

        def scores(t):
            t["qd_t"] = qdt_ref[:, pl.ds(t["at"], tile)]
            rhs = spread(t["qd_t"])
            t["near"], t["far"] = mm(kv_ref[t["win"], :], rhs), mm(mkv, rhs)

        def softmax(t):
            s_near = jnp.where(
                usable(t["at"], 2 * tile, length), t["near"][:, 0:128] + tb_ref[...], NEG_BIG
            )
            s_far = t["far"][:, 0:128]
            high = jnp.maximum(
                jnp.max(s_near, axis=0, keepdims=True), jnp.max(s_far, axis=0, keepdims=True)
            )
            e_near, e_far = jnp.exp(s_near - high), jnp.exp(s_far - high)
            inv = 1.0 / (
                jnp.sum(e_near, axis=0, keepdims=True) + jnp.sum(e_far, axis=0, keepdims=True)
            )
            t["p_near"], t["p_far"] = e_near * inv, e_far * inv
            t["pb_near"], t["pb_far"] = t["p_near"].astype(BF16), t["p_far"].astype(BF16)

        def forward(t):
            out = mm(kvt_ref[64:128, t["win"]], t["pb_near"]) + mm(mkv_t[64:128], t["pb_far"])
            t["out"] = out.astype(BF16).astype(F32)

        def score_grads(t):
            row_dot = jnp.sum(t["qd_t"][64:128].astype(F32) * t["out"], axis=0, keepdims=True)
            ds_near = t["p_near"] * (t["near"][:, 128:256] - row_dot)
            ds_far = t["p_far"] * (t["far"][:, 128:256] - row_dot)
            t["bias"] += ds_near
            t["db_near"], t["db_far"] = ds_near.astype(BF16), ds_far.astype(BF16)

        def backward(t):
            back = stack(qd_ref[pl.ds(t["at"], tile), :])
            dq = mm(kvt_ref[0:64, t["win"]], t["db_near"]) + mm(mkv_t[0:64], t["db_far"])
            t["dq"] = dq * scale
            t["d_near"] = mm(side(t["db_near"], t["pb_near"]), back)
            t["d_far"] = mm(side(t["db_far"], t["pb_far"]), back)

        def write(t):
            d, o = t["dq"], t["out"]
            if t["first_half"]:
                placed = mm(mem_rows, pick_ref[:, pl.ds(t["at"], tile)])
                o = jnp.where(placed[192:193] > 0.5, placed[64:128], o)
                d = d + (placed[0:64] + placed[128:192])
            o = jnp.where(lane[0:1] + t["at"] < length, o, 0.0)
            y_ref[t["slot"], 0:tile, 128:256] = jnp.concatenate([d, o], axis=0).astype(BF16).T

        stages = (scores, softmax, forward, score_grads, backward, write)

        def band(first_half, i, c):
            tiles = []
            bias, tail, far = gb_ref[...], 0.0, gm_ref[...]
            for u in range(BAND_GROUP):
                slot = i * BAND_GROUP + u
                at = aligned(slot * tile, tile)
                half = slot < slots // 2 if first_half is None else first_half
                tiles.append({"slot": slot, "at": at, "win": pl.ds(at, 2 * tile), "first_half": half})
            for step in range(BAND_GROUP + SKEW * (len(stages) - 1)):
                for k, stage in enumerate(stages):
                    u = step - SKEW * k
                    if not 0 <= u < BAND_GROUP:
                        continue
                    t = tiles[u]
                    if stage is score_grads:
                        t["bias"] = bias
                    stage(t)
                    if stage is score_grads:
                        bias = t["bias"]
                    if stage is backward:
                        ww_ref[pl.ds(t["at"], tile), 0:128] += tail + t["d_near"][0:tile]
                        tail = t["d_near"][tile:]
                        far = far + t["d_far"]
            ww_ref[pl.ds(aligned(tiles[-1]["at"] + tile, tile), tile), 0:128] += tail
            gb_ref[...] = bias
            gm_ref[...] = far
            return c

        rounds = slots // BAND_GROUP
        if rounds == 1:
            band(None, 0, 0)
        else:
            repeat(0, rounds // 2, functools.partial(band, True), 0)
            repeat(rounds // 2, rounds, functools.partial(band, False), 0)

        wide_bias = jnp.concatenate([gb_ref[...], jnp.zeros((128, 128), F32)], axis=0).T
        bias_sum = jnp.sum(shear(wide_bias, blk - 1, -1), axis=0, keepdims=True)[:, 0:256]
        b0 = bias_sum.astype(BF16).astype(F32)
        b1 = (bias_sum - b0).astype(BF16).astype(F32)
        b2 = bias_sum - b0 - b1
        bias_rows = jnp.concatenate(
            [b0, b1, b2, jnp.zeros((BIAS_ROWS - 3, 256), F32)], axis=0
        ).astype(BF16)

        mem_back = jnp.concatenate(split2(gm_ref[...]), axis=0)

        def finish(first_half):
            def body(i, c):
                at = aligned(i * chunk, chunk)
                grads = ww_ref[pl.ds(aligned(at + blk, blk), chunk), 0:128]
                if first_half:
                    pick = (wide_row == wide_sub + at).astype(BF16)
                    grads = grads + mm(side(pick, pick), mem_back)
                y_ref[pl.ds(i * GROUP, GROUP), 0:tile, 0:128] = grads.astype(BF16).reshape(
                    GROUP, tile, 128
                )
                for u in range(GROUP):
                    y_ref[i * GROUP + u, tile:, :] = bias_rows
                return c

            return body

        repeat(0, steps // 2, finish(True), 0)
        repeat(steps // 2, steps, finish(False), 0)


def vmem(shape, dtype):
    return pltpu.VMEM(shape, dtype)


def grant(frames):
    return pltpu.CompilerParams(vmem_limit_bytes=min(16 * frames // 2048, 60) * 1024 * 1024)


def core_call(by_head, rows, position_bias):
    slots, tile, _ = by_head.shape
    frames = slots * tile
    return pl.pallas_call(
        core_kernel,
        out_shape=jax.ShapeDtypeStruct((slots, tile + BIAS_ROWS, 256), BF16),
        scratch_shapes=[
            vmem((frames + tile, 128), BF16),
            vmem((128, frames + tile), BF16),
            vmem((frames, 128), BF16),
            vmem((128, frames), BF16),
            vmem((frames + tile, 256), F32),
            vmem((2 * tile, 128), F32),
            vmem((2 * tile, 128), F32),
            vmem((128, 128), F32),
            vmem((128, frames // 2), BF16),
        ],
        compiler_params=grant(frames),
    )(rows, position_bias, by_head)


def local(
    frame_queries, frame_keys, frame_values, cotangent, frame_mask, global_rows, position_bias
):
    slots = lax.axis_size("seq")
    tile, width = frame_queries.shape
    heads, span = position_bias.shape
    memory = global_rows.shape[0]
    frames = slots * tile

    hbm = pl.BlockSpec(memory_space=pltpu.MemorySpace.HBM)
    whole = pltpu.VMEM((tile, width), BF16)
    packed = pl.pallas_call(
        pack_kernel,
        out_shape=jax.ShapeDtypeStruct((slots, tile, 256), BF16),
        in_specs=[hbm] * 5,
        scratch_shapes=[
            pltpu.VMEM((1, tile), jnp.int32),
            whole,
            whole,
            whole,
            whole,
            pltpu.SemaphoreType.DMA((5,)),
        ],
        compiler_params=grant(frames),
    )(
        *(
            pltpu.with_memory_space_constraint(x, pltpu.MemorySpace.HBM)
            for x in (
                frame_mask.reshape(1, tile),
                frame_keys,
                frame_values,
                frame_queries,
                cotangent,
            )
        )
    )
    by_head = lax.all_to_all(packed, "seq", 0, 0, tiled=True)
    grads = core_call(by_head, global_rows.reshape(1, memory), position_bias)
    by_frame = lax.all_to_all(grads, "seq", 0, 0, tiled=True)
    rows = jax.ShapeDtypeStruct((tile, width), BF16)
    attended, dq, dk, dv, grad_bias = pl.pallas_call(
        unpack_kernel,
        out_shape=(rows, rows, rows, rows, jax.ShapeDtypeStruct((heads, span), F32)),
        compiler_params=grant(frames),
    )(by_frame)
    return (attended, dq, dk, dv, grad_bias)


def solution(mesh):
    return jax.shard_map(
        local,
        mesh=mesh,
        in_specs=(
            P(("groups", "seq"), None),
            P(("groups", "seq"), None),
            P(("groups", "seq"), None),
            P(("groups", "seq"), None),
            P(("groups", "seq")),
            P("groups"),
            P(),
        ),
        out_specs=(
            P(("groups", "seq"), None),
            P(("groups", "seq"), None),
            P(("groups", "seq"), None),
            P(("groups", "seq"), None),
            P("groups", None),
        ),
        check_vma=False,
    )
```

```python
import functools

import jax
import jax.numpy as jnp
from jax import lax
from jax.experimental import pallas as pl
from jax.experimental.pallas import tpu as pltpu
from jax.sharding import PartitionSpec as P

NEG_BIG = -1e30
DEAD = 64.0
BIAS_ROWS = 8
GROUP = 8
BAND_GROUP = 16
SKEW = 4
WIDE_FIRST = 0
WIDE_TILES = 4
WIDE_STEP = 5
BF16 = jnp.bfloat16
F32 = jnp.float32


def mm(a, b):
    return jnp.dot(a, b, preferred_element_type=F32)


def split2(x):
    high = x.astype(BF16)
    return high, (x - high.astype(F32)).astype(BF16)


def iota(shape, dim):
    return lax.broadcasted_iota(jnp.int32, shape, dim)


def swap_halves(x):
    half = x.shape[1] // 2
    return jnp.concatenate([x[:, half:], x[:, :half]], axis=1)


def pack_kernel(*refs):
    sources, out_ref, held, sem = refs[:5], refs[5], refs[6:11], refs[11]
    copies = [
        pltpu.make_async_copy(source, here, sem.at[i])
        for i, (source, here) in enumerate(zip(sources, held))
    ]
    for copy in copies:
        copy.start()
    mask_ref, k_ref, v_ref, q_ref, g_ref = held
    slots, rows, _ = out_ref.shape
    pairs = q_ref.shape[1] // 128
    low = iota((rows, 128), 1) < 64

    @pl.loop(2 * pairs, slots)
    def _(s):
        out_ref[s] = jnp.zeros(out_ref.shape[1:], BF16)

    for copy in copies[:3]:
        copy.wait()
    for i in range(pairs):
        at = slice(128 * i, 128 * (i + 1))
        k, v = k_ref[:, at], v_ref[:, at]
        out_ref[2 * i, :, 0:128] = jnp.where(low, k, swap_halves(v))
        out_ref[2 * i + 1, :, 0:128] = jnp.where(low, swap_halves(k), v)
    for copy in copies[3:]:
        copy.wait()
    alive = iota((rows, 128), 0) < jnp.sum(mask_ref[...])
    for i in range(pairs):
        at = slice(128 * i, 128 * (i + 1))
        q, g = q_ref[:, at], jnp.where(alive, g_ref[:, at], jnp.asarray(DEAD, BF16))
        out_ref[2 * i, :, 128:256] = jnp.where(low, q, swap_halves(g))
        out_ref[2 * i + 1, :, 128:256] = jnp.where(low, swap_halves(q), g)


def unpack_kernel(in_ref, att_ref, dq_ref, dk_ref, dv_ref, gb_ref):
    rows = att_ref.shape[0]
    pairs = att_ref.shape[1] // 128
    low = iota((rows, 128), 1) < 64
    for i in range(pairs):
        at = slice(128 * i, 128 * (i + 1))
        a, b = in_ref[2 * i, :rows, 0:128], in_ref[2 * i + 1, :rows, 0:128]
        dk_ref[:, at] = jnp.where(low, a, swap_halves(b))
        dv_ref[:, at] = jnp.where(low, swap_halves(a), b)
        a, b = in_ref[2 * i, :rows, 128:256], in_ref[2 * i + 1, :rows, 128:256]
        dq_ref[:, at] = jnp.where(low, a, swap_halves(b))
        att_ref[:, at] = jnp.where(low, swap_halves(a), b)
    for h in range(2 * pairs):
        parts = in_ref[h, rows:, :].astype(F32)
        whole = parts[0:1] + parts[1:2] + parts[2:3]
        gb_ref[h : h + 1, :] = whole[:, : gb_ref.shape[1]]


def repeat(first, last, body, carry):
    if last - first > 2:
        return lax.fori_loop(first, last, body, carry)
    for i in range(first, last):
        carry = body(i, carry)
    return carry


def aligned(x, size):
    return x if isinstance(x, int) else pl.multiple_of(x, size)


def shear(x, first, step):
    rows, lanes = x.shape
    row = iota(x.shape, 0)
    x = pltpu.roll(x, first % lanes, 1)
    bit = 1
    while bit < rows:
        x = jnp.where((row & bit) != 0, pltpu.roll(x, (step * bit) % lanes, 1), x)
        bit *= 2
    return x


def core_kernel(
    rows_ref, bias_ref, x_ref, y_ref, kv_ref, kvt_ref, qdt_ref, ww_ref, tb_ref, gb_ref, gm_ref, pick_ref, keep_ref
):
    slots, tile, _ = x_ref.shape
    frames = slots * tile
    blk = tile // 2
    heads, span = bias_ref.shape
    memory = rows_ref.shape[1]
    scale = 64 ** (-0.5)
    owner = lax.axis_index("seq")
    chunk = GROUP * tile
    steps = slots // GROUP

    @pl.when(owner < heads)
    def _():
        lane = iota((128, 128), 1)
        sub = iota((128, 128), 0)
        low_lane = lane < 64
        low_row = sub < 64
        gr_row = jnp.broadcast_to(rows_ref[...], (128, memory))
        gr_col = gr_row.T
        zero_t = jnp.zeros((128, 128), BF16)

        def side(top, bottom):
            return jnp.concatenate([top, bottom], axis=1)

        def spread(x_t):
            return side(jnp.where(low_row, x_t, zero_t), jnp.where(low_row, zero_t, x_t))

        def stack(x):
            return jnp.concatenate(
                [jnp.where(low_lane, x, zero_t), jnp.where(low_lane, zero_t, x)], axis=0
            )

        def over_rows(body, carry):
            carry = repeat(
                0, steps - 1, lambda i, c: body(aligned(i * chunk, chunk), chunk, c), carry
            )
            return body(frames - chunk, chunk + tile, carry)

        def usable(at, rows, length):
            place = iota((rows, 128), 0) + (at - blk)
            inside = place < length
            if isinstance(at, int) and at >= blk:
                return inside
            return (place >= 0) & inside

        zeros = jnp.zeros((blk, 128), BF16)
        kv_ref[0:blk, :] = zeros
        kv_ref[frames + blk :, :] = zeros
        wide_sub = iota((chunk, 128), 0)
        wide_lane = iota((128, chunk), 1)
        wide_row = jnp.broadcast_to(gr_row[0:1], (chunk, memory))
        wide_col = jnp.concatenate([gr_col] * GROUP, axis=1)
        ones = jnp.ones((16, memory), BF16)
        scales = jnp.where(iota((1, 128), 1) < 64, scale, 1.0).astype(BF16)

        def prepare(first_half):
            def body(i, c):
                count, mem = c
                at = aligned(i * chunk, chunk)
                x = x_ref[pl.ds(i * GROUP, GROUP)].reshape(chunk, 256)
                kv_ref[pl.ds(aligned(at + blk, blk), chunk), :] = x[:, 0:128]
                qd_t = (x[:, 128:256] * scales).T
                qdt_ref[:, pl.ds(at, chunk)] = qd_t
                alive = (qd_t[64:80].astype(F32)[0:1] < 0.5 * DEAD).astype(F32)
                if first_half:
                    pick = (wide_col == wide_lane + at).astype(BF16)
                    pick_ref[:, pl.ds(at, chunk)] = pick
                    mem = mem + mm(pick, x)
                    keep_ref[:, pl.ds(at, chunk)] = alive - mm(ones, pick)[0:1]
                else:
                    keep_ref[:, pl.ds(at, chunk)] = alive
                return count + jnp.sum(alive, axis=1, keepdims=True), mem

            return body

        carry = (jnp.zeros((1, 1), F32), jnp.zeros((128, 256), F32))
        carry = repeat(0, steps // 2, prepare(True), carry)
        count, mem = repeat(steps // 2, steps, prepare(False), carry)
        length = count.astype(jnp.int32)
        mkv = mem[:, 0:128].astype(BF16)
        mqo = jnp.where(low_lane, mem[:, 128:256] * scale, mem[:, 128:256]).astype(BF16)
        mkv_t = mkv.T
        mqo_t = mqo.T

        head = jnp.minimum(owner, heads - 1)
        b_row = side(bias_ref[pl.ds(head, 1), :], jnp.zeros((1, 384 - span), F32))
        table = shear(jnp.broadcast_to(b_row, (128, 384)), 1 - blk, 1)[:, : 2 * tile].T
        gap = iota(table.shape, 0) // blk - iota(table.shape, 1) // blk
        tb_ref[...] = jnp.where((gap >= 0) & (gap <= 2), table, NEG_BIG)
        gb_ref[...] = jnp.zeros_like(gb_ref)
        gm_ref[...] = jnp.zeros_like(gm_ref)

        wide_rhs = spread(mqo_t)
        wide_back = stack(mqo)

        def wide_scores(at, rows, top):
            kv = kv_ref[pl.ds(at, rows), :]
            kvt_ref[:, pl.ds(at, rows)] = kv.T
            both = mm(kv, wide_rhs)
            w = jnp.where(usable(at, rows, length), both[:, 0:128], NEG_BIG)
            ww_ref[pl.ds(at, rows), 0:128] = w
            ww_ref[pl.ds(at, rows), 128:256] = both[:, 128:256]
            return jnp.maximum(top, jnp.max(w, axis=0, keepdims=True))

        def wide_sums(at, rows, c):
            total, numer = c
            e = jnp.exp(ww_ref[pl.ds(at, rows), 0:128] - wide["top"])
            ww_ref[pl.ds(at, rows), 0:128] = e
            high, rest = split2(e)
            numer = numer + mm(kvt_ref[64:128, pl.ds(at, rows)], side(high, rest))
            return total + jnp.sum(e, axis=0, keepdims=True), numer

        def wide_out():
            total, numer = wide["sums"]
            mem_out = ((numer[:, 0:128] + numer[:, 128:256]) / total).astype(BF16)
            wide["out"] = mem_out
            wide["dot"] = jnp.sum(
                mqo_t[64:128].astype(F32) * mem_out.astype(F32), axis=0, keepdims=True
            )
            wide["share"] = 1.0 / total

        def wide_grads(at, rows, dq):
            p = ww_ref[pl.ds(at, rows), 0:128] * wide["share"]
            dw = (p * (ww_ref[pl.ds(at, rows), 128:256] - wide["dot"])).astype(BF16)
            ww_ref[pl.ds(at, rows), 0:128] = mm(side(dw, p.astype(BF16)), wide_back)
            return dq + mm(kvt_ref[0:64, pl.ds(at, rows)], dw)

        def wide_rows():
            high, rest = split2(wide["dq"] * scale)
            wide["rows"] = jnp.concatenate([high, wide["out"], rest], axis=0)

        wide = {
            "top": jnp.full((1, 128), NEG_BIG, F32),
            "sums": (jnp.zeros((1, 128), F32), jnp.zeros((64, 256), F32)),
            "dq": jnp.zeros((64, 128), F32),
        }
        passes = (("top", wide_scores, None), ("sums", wide_sums, wide_out), ("dq", wide_grads, wide_rows))

        def scores(t):
            t["qd_t"] = qdt_ref[:, pl.ds(t["at"], tile)]
            rhs = spread(t["qd_t"])
            t["near"], t["far"] = mm(kv_ref[t["win"], :], rhs), mm(mkv, rhs)

        def softmax(t):
            s_near = jnp.where(
                usable(t["at"], 2 * tile, length), t["near"][:, 0:128] + tb_ref[...], NEG_BIG
            )
            s_far = t["far"][:, 0:128]
            high = jnp.maximum(
                jnp.max(s_near, axis=0, keepdims=True), jnp.max(s_far, axis=0, keepdims=True)
            )
            e_near, e_far = jnp.exp(s_near - high), jnp.exp(s_far - high)
            inv = keep_ref[:, pl.ds(t["at"], tile)] / (
                jnp.sum(e_near, axis=0, keepdims=True) + jnp.sum(e_far, axis=0, keepdims=True)
            )
            t["p_near"], t["p_far"] = e_near * inv, e_far * inv
            t["pb_near"], t["pb_far"] = t["p_near"].astype(BF16), t["p_far"].astype(BF16)

        def forward(t):
            out = mm(kvt_ref[64:128, t["win"]], t["pb_near"]) + mm(mkv_t[64:128], t["pb_far"])
            t["out"] = out.astype(BF16).astype(F32)

        def score_grads(t):
            row_dot = jnp.sum(t["qd_t"][64:128].astype(F32) * t["out"], axis=0, keepdims=True)
            ds_near = t["p_near"] * (t["near"][:, 128:256] - row_dot)
            ds_far = t["p_far"] * (t["far"][:, 128:256] - row_dot)
            t["bias"] += ds_near
            t["db_near"], t["db_far"] = ds_near.astype(BF16), ds_far.astype(BF16)

        def backward(t):
            back = stack(x_ref[t["slot"], :, 128:256] * scales)
            dq = mm(kvt_ref[0:64, t["win"]], t["db_near"]) + mm(mkv_t[0:64], t["db_far"])
            t["dq"] = dq * scale
            t["d_near"] = mm(side(t["db_near"], t["pb_near"]), back)
            t["d_far"] = mm(side(t["db_far"], t["pb_far"]), back)

        def write(t):
            d, o = t["dq"], t["out"]
            if t["first_half"]:
                placed = mm(wide["rows"], pick_ref[:, pl.ds(t["at"], tile)])
                o = o + placed[64:128]
                d = d + (placed[0:64] + placed[128:192])
            y_ref[t["slot"], 0:tile, 128:256] = jnp.concatenate([d, o], axis=0).astype(BF16).T

        stages = (scores, softmax, forward, score_grads, backward, write)

        def band(first_half, between, i, c):
            tiles = []
            bias, tail, far = gb_ref[...], 0.0, gm_ref[...]
            for u in range(BAND_GROUP):
                slot = i * BAND_GROUP + u
                at = aligned(slot * tile, tile)
                half = slot < slots // 2 if first_half is None else first_half
                tiles.append({"slot": slot, "at": at, "win": pl.ds(at, 2 * tile), "first_half": half})
            for step in range(BAND_GROUP + SKEW * (len(stages) - 1)):
                for work in between.get(step, ()):
                    work()
                for k, stage in enumerate(stages):
                    u = step - SKEW * k
                    if not 0 <= u < BAND_GROUP:
                        continue
                    t = tiles[u]
                    if stage is score_grads:
                        t["bias"] = bias
                    stage(t)
                    if stage is score_grads:
                        bias = t["bias"]
                    if stage is backward:
                        ww_ref[pl.ds(t["at"], tile), 0:128] += tail + t["d_near"][0:tile]
                        tail = t["d_near"][tile:]
                        far = far + t["d_far"]
            ww_ref[pl.ds(aligned(tiles[-1]["at"] + tile, tile), tile), 0:128] += tail
            gb_ref[...] = bias
            gm_ref[...] = far
            return c

        rounds = slots // BAND_GROUP
        if rounds == 1:
            between = {}
            part = WIDE_TILES * tile
            cuts = list(range(0, frames, part))
            for k, (name, body, after) in enumerate(passes):
                for j, at in enumerate(cuts):

                    def work(name=name, body=body, at=at, last=j == len(cuts) - 1, after=after):
                        wide[name] = body(at, part + tile if last else part, wide[name])
                        if last and after is not None:
                            after()

                    step = WIDE_FIRST + k * WIDE_STEP + j * WIDE_STEP // len(cuts)
                    between.setdefault(step, []).append(work)
            band(None, between, 0, 0)
        else:
            for name, body, after in passes:
                wide[name] = over_rows(body, wide[name])
                if after is not None:
                    after()
            repeat(0, rounds // 2, functools.partial(band, True, {}), 0)
            repeat(rounds // 2, rounds, functools.partial(band, False, {}), 0)

        wide_bias = jnp.concatenate([gb_ref[...], jnp.zeros((128, 128), F32)], axis=0).T
        bias_sum = jnp.sum(shear(wide_bias, blk - 1, -1), axis=0, keepdims=True)[:, 0:256]
        b0 = bias_sum.astype(BF16).astype(F32)
        b1 = (bias_sum - b0).astype(BF16).astype(F32)
        b2 = bias_sum - b0 - b1
        bias_rows = jnp.concatenate(
            [b0, b1, b2, jnp.zeros((BIAS_ROWS - 3, 256), F32)], axis=0
        ).astype(BF16)

        mem_back = jnp.concatenate(split2(gm_ref[...]), axis=0)

        def finish(first_half):
            def body(i, c):
                at = aligned(i * chunk, chunk)
                grads = ww_ref[pl.ds(aligned(at + blk, blk), chunk), 0:128]
                if first_half:
                    pick = (wide_row == wide_sub + at).astype(BF16)
                    grads = grads + mm(side(pick, pick), mem_back)
                y_ref[pl.ds(i * GROUP, GROUP), 0:tile, 0:128] = grads.astype(BF16).reshape(
                    GROUP, tile, 128
                )
                for u in range(GROUP):
                    y_ref[i * GROUP + u, tile:, :] = bias_rows
                return c

            return body

        repeat(0, steps // 2, finish(True), 0)
        repeat(steps // 2, steps, finish(False), 0)


def vmem(shape, dtype):
    return pltpu.VMEM(shape, dtype)


def grant(frames):
    return pltpu.CompilerParams(vmem_limit_bytes=min(16 * frames // 2048, 60) * 1024 * 1024)


def core_call(by_head, rows, position_bias):
    slots, tile, _ = by_head.shape
    frames = slots * tile
    return pl.pallas_call(
        core_kernel,
        out_shape=jax.ShapeDtypeStruct((slots, tile + BIAS_ROWS, 256), BF16),
        scratch_shapes=[
            vmem((frames + tile, 128), BF16),
            vmem((128, frames + tile), BF16),
            vmem((128, frames), BF16),
            vmem((frames + tile, 256), F32),
            vmem((2 * tile, 128), F32),
            vmem((2 * tile, 128), F32),
            vmem((128, 128), F32),
            vmem((128, frames // 2), BF16),
            vmem((1, frames), F32),
        ],
        compiler_params=grant(frames),
    )(rows, position_bias, by_head)


def local(
    frame_queries, frame_keys, frame_values, cotangent, frame_mask, global_rows, position_bias
):
    slots = lax.axis_size("seq")
    tile, width = frame_queries.shape
    heads, span = position_bias.shape
    memory = global_rows.shape[0]
    frames = slots * tile

    hbm = pl.BlockSpec(memory_space=pltpu.MemorySpace.HBM)
    whole = pltpu.VMEM((tile, width), BF16)
    packed = pl.pallas_call(
        pack_kernel,
        out_shape=jax.ShapeDtypeStruct((slots, tile, 256), BF16),
        in_specs=[hbm] * 5,
        scratch_shapes=[
            pltpu.VMEM((1, tile), jnp.int32),
            whole,
            whole,
            whole,
            whole,
            pltpu.SemaphoreType.DMA((5,)),
        ],
        compiler_params=grant(frames),
    )(
        *(
            pltpu.with_memory_space_constraint(x, pltpu.MemorySpace.HBM)
            for x in (
                frame_mask.reshape(1, tile),
                frame_keys,
                frame_values,
                frame_queries,
                cotangent,
            )
        )
    )
    by_head = lax.all_to_all(packed, "seq", 0, 0, tiled=True)
    grads = core_call(by_head, global_rows.reshape(1, memory), position_bias)
    by_frame = lax.all_to_all(grads, "seq", 0, 0, tiled=True)
    rows = jax.ShapeDtypeStruct((tile, width), BF16)
    attended, dq, dk, dv, grad_bias = pl.pallas_call(
        unpack_kernel,
        out_shape=(rows, rows, rows, rows, jax.ShapeDtypeStruct((heads, span), F32)),
        compiler_params=grant(frames),
    )(by_frame)
    return (attended, dq, dk, dv, grad_bias)


def solution(mesh):
    return jax.shard_map(
        local,
        mesh=mesh,
        in_specs=(
            P(("groups", "seq"), None),
            P(("groups", "seq"), None),
            P(("groups", "seq"), None),
            P(("groups", "seq"), None),
            P(("groups", "seq")),
            P("groups"),
            P(),
        ),
        out_specs=(
            P(("groups", "seq"), None),
            P(("groups", "seq"), None),
            P(("groups", "seq"), None),
            P(("groups", "seq"), None),
            P("groups", None),
        ),
        check_vma=False,
    )
```

```python
import functools

import jax
import jax.numpy as jnp
from jax import lax
from jax.experimental import pallas as pl
from jax.experimental.pallas import tpu as pltpu
from jax.sharding import PartitionSpec as P

NEG_BIG = -1e30
DEAD = 64.0
BIAS_ROWS = 8
GROUP = 8
BAND_GROUP = 16
SKEW = 4
WIDE_FIRST = 0
WIDE_TILES = 2
WIDE_STEP = 5
BF16 = jnp.bfloat16
F32 = jnp.float32


def mm(a, b):
    return jnp.dot(a, b, preferred_element_type=F32)


def split2(x):
    high = x.astype(BF16)
    return high, (x - high.astype(F32)).astype(BF16)


def iota(shape, dim):
    return lax.broadcasted_iota(jnp.int32, shape, dim)


def swap_halves(x):
    half = x.shape[1] // 2
    return jnp.concatenate([x[:, half:], x[:, :half]], axis=1)


def pack_kernel(*refs):
    sources, out_ref, held, sem = refs[:5], refs[5], refs[6:11], refs[11]
    copies = [
        pltpu.make_async_copy(source, here, sem.at[i])
        for i, (source, here) in enumerate(zip(sources, held))
    ]
    for copy in copies:
        copy.start()
    mask_ref, k_ref, v_ref, q_ref, g_ref = held
    slots, rows, _ = out_ref.shape
    pairs = q_ref.shape[1] // 128
    low = iota((rows, 128), 1) < 64

    @pl.loop(2 * pairs, slots)
    def _(s):
        out_ref[s] = jnp.zeros(out_ref.shape[1:], BF16)

    for copy in copies[:3]:
        copy.wait()
    for i in range(pairs):
        at = slice(128 * i, 128 * (i + 1))
        even, odd = 2 * i, 2 * i + 1
        k, v = k_ref[:, at], v_ref[:, at]
        out_ref[even, :, 0:128] = jnp.where(low, k, swap_halves(v))
        out_ref[odd, :, 0:128] = jnp.where(low, swap_halves(k), v)
    for copy in copies[3:]:
        copy.wait()
    alive = iota((rows, 128), 0) < jnp.sum(mask_ref[...])
    for i in range(pairs):
        at = slice(128 * i, 128 * (i + 1))
        q, g = q_ref[:, at], jnp.where(alive, g_ref[:, at], jnp.asarray(DEAD, BF16))
        even, odd = 2 * i, 2 * i + 1
        out_ref[even, :, 128:256] = jnp.where(low, q, swap_halves(g))
        out_ref[odd, :, 128:256] = jnp.where(low, swap_halves(q), g)


def unpack_kernel(in_ref, att_ref, dq_ref, dk_ref, dv_ref, gb_ref):
    rows = att_ref.shape[0]
    pairs = att_ref.shape[1] // 128
    low = iota((rows, 128), 1) < 64
    for i in range(pairs):
        at = slice(128 * i, 128 * (i + 1))
        even, odd = 2 * i, 2 * i + 1
        a, b = in_ref[even, :rows, :], in_ref[odd, :rows, :]
        dk_ref[:, at] = jnp.where(low, a, swap_halves(b))
        dv_ref[:, at] = jnp.where(low, swap_halves(a), b)
        a, b = in_ref[even, rows : 2 * rows, :], in_ref[odd, rows : 2 * rows, :]
        dq_ref[:, at] = jnp.where(low, a, swap_halves(b))
        att_ref[:, at] = jnp.where(low, swap_halves(a), b)
    for h in range(2 * pairs):
        parts = in_ref[h, 2 * rows :, :].astype(F32)
        whole = parts[0:2] + parts[2:4] + parts[4:6]
        whole = jnp.concatenate([whole[0:1], whole[1:2]], axis=1)
        gb_ref[h : h + 1, :] = whole[:, : gb_ref.shape[1]]


def repeat(first, last, body, carry):
    if last - first > 2:
        return lax.fori_loop(first, last, body, carry)
    for i in range(first, last):
        carry = body(i, carry)
    return carry


def aligned(x, size):
    return x if isinstance(x, int) else pl.multiple_of(x, size)


def shear(x, first, step):
    rows, lanes = x.shape
    row = iota(x.shape, 0)
    x = pltpu.roll(x, first % lanes, 1)
    bit = 1
    while bit < rows:
        x = jnp.where((row & bit) != 0, pltpu.roll(x, (step * bit) % lanes, 1), x)
        bit *= 2
    return x


def core_kernel(
    rows_ref, bias_ref, x_ref, y_ref, kv_ref, kvt_ref, qdt_ref, ww_ref, tb_ref, gb_ref, gm_ref, pick_ref, keep_ref
):
    slots, tile, _ = x_ref.shape
    frames = slots * tile
    blk = tile // 2
    heads, span = bias_ref.shape
    memory = rows_ref.shape[1]
    scale = 64 ** (-0.5)
    owner = lax.axis_index("seq")
    chunk = GROUP * tile
    steps = slots // GROUP

    @pl.when(owner < heads)
    def _():
        lane = iota((128, 128), 1)
        sub = iota((128, 128), 0)
        low_lane = lane < 64
        low_row = sub < 64
        gr_row = jnp.broadcast_to(rows_ref[...], (128, memory))
        gr_col = gr_row.T
        zero_t = jnp.zeros((128, 128), BF16)

        def side(top, bottom):
            return jnp.concatenate([top, bottom], axis=1)

        def spread(x_t):
            return side(jnp.where(low_row, x_t, zero_t), jnp.where(low_row, zero_t, x_t))

        def stack(x):
            return jnp.concatenate(
                [jnp.where(low_lane, x, zero_t), jnp.where(low_lane, zero_t, x)], axis=0
            )

        def over_rows(body, carry):
            carry = repeat(
                0, steps - 1, lambda i, c: body(aligned(i * chunk, chunk), chunk, c), carry
            )
            return body(frames - chunk, chunk + tile, carry)

        def usable(at, rows, length):
            place = iota((rows, 128), 0) + (at - blk)
            inside = place < length
            if isinstance(at, int) and at >= blk:
                return inside
            return (place >= 0) & inside

        zeros = jnp.zeros((blk, 128), BF16)
        kv_ref[0:blk, :] = zeros
        kv_ref[frames + blk :, :] = zeros
        wide_sub = iota((chunk, 128), 0)
        wide_lane = iota((128, chunk), 1)
        wide_row = jnp.broadcast_to(gr_row[0:1], (chunk, memory))
        wide_col = jnp.concatenate([gr_col] * GROUP, axis=1)
        ones = jnp.ones((16, memory), BF16)
        scales = jnp.where(iota((1, 128), 1) < 64, scale, 1.0).astype(BF16)

        def prepare(first_half):
            def body(i, c):
                count, mem = c
                at = aligned(i * chunk, chunk)
                x = x_ref[pl.ds(i * GROUP, GROUP)].reshape(chunk, 256)
                kv_ref[pl.ds(aligned(at + blk, blk), chunk), :] = x[:, 0:128]
                qd_t = (x[:, 128:256] * scales).T
                qdt_ref[:, pl.ds(at, chunk)] = qd_t
                alive = (qd_t[64:80].astype(F32)[0:1] < 0.5 * DEAD).astype(F32)
                if first_half:
                    pick = (wide_col == wide_lane + at).astype(BF16)
                    pick_ref[:, pl.ds(at, chunk)] = pick
                    mem = mem + mm(pick, x)
                    keep_ref[:, pl.ds(at, chunk)] = alive - mm(ones, pick)[0:1]
                else:
                    keep_ref[:, pl.ds(at, chunk)] = alive
                return count + jnp.sum(alive, axis=1, keepdims=True), mem

            return body

        carry = (jnp.zeros((1, 1), F32), jnp.zeros((128, 256), F32))
        carry = repeat(0, steps // 2, prepare(True), carry)
        count, mem = repeat(steps // 2, steps, prepare(False), carry)
        length = count.astype(jnp.int32)
        mkv = mem[:, 0:128].astype(BF16)
        mqo = jnp.where(low_lane, mem[:, 128:256] * scale, mem[:, 128:256]).astype(BF16)
        mkv_t = mkv.T
        mqo_t = mqo.T

        head = jnp.minimum(owner, heads - 1)
        b_row = side(bias_ref[pl.ds(head, 1), :], jnp.zeros((1, 384 - span), F32))
        table = shear(jnp.broadcast_to(b_row, (128, 384)), 1 - blk, 1)[:, : 2 * tile].T
        gap = iota(table.shape, 0) // blk - iota(table.shape, 1) // blk
        tb_ref[...] = jnp.where((gap >= 0) & (gap <= 2), table, NEG_BIG)
        gb_ref[...] = jnp.zeros_like(gb_ref)
        gm_ref[...] = jnp.zeros_like(gm_ref)

        wide_rhs = spread(mqo_t)
        wide_back = stack(mqo)

        def wide_scores(at, rows, top):
            kv = kv_ref[pl.ds(at, rows), :]
            kvt_ref[:, pl.ds(at, rows)] = kv.T
            both = mm(kv, wide_rhs)
            w = jnp.where(usable(at, rows, length), both[:, 0:128], NEG_BIG)
            ww_ref[pl.ds(at, rows), 0:128] = w
            ww_ref[pl.ds(at, rows), 128:256] = both[:, 128:256]
            return jnp.maximum(top, jnp.max(w, axis=0, keepdims=True))

        def wide_sums(at, rows, c):
            total, numer = c
            e = jnp.exp(ww_ref[pl.ds(at, rows), 0:128] - wide["top"])
            ww_ref[pl.ds(at, rows), 0:128] = e
            high, rest = split2(e)
            numer = numer + mm(kvt_ref[64:128, pl.ds(at, rows)], side(high, rest))
            return total + jnp.sum(e, axis=0, keepdims=True), numer

        def wide_out():
            total, numer = wide["sums"]
            mem_out = ((numer[:, 0:128] + numer[:, 128:256]) / total).astype(BF16)
            wide["out"] = mem_out
            wide["dot"] = jnp.sum(
                mqo_t[64:128].astype(F32) * mem_out.astype(F32), axis=0, keepdims=True
            )
            wide["share"] = 1.0 / total

        def wide_grads(at, rows, dq):
            p = ww_ref[pl.ds(at, rows), 0:128] * wide["share"]
            dw = (p * (ww_ref[pl.ds(at, rows), 128:256] - wide["dot"])).astype(BF16)
            ww_ref[pl.ds(at, rows), 0:128] = mm(side(dw, p.astype(BF16)), wide_back)
            return dq + mm(kvt_ref[0:64, pl.ds(at, rows)], dw)

        def wide_rows():
            high, rest = split2(wide["dq"] * scale)
            wide["rows"] = jnp.concatenate([high, wide["out"], rest], axis=0)

        wide = {
            "top": jnp.full((1, 128), NEG_BIG, F32),
            "sums": (jnp.zeros((1, 128), F32), jnp.zeros((64, 256), F32)),
            "dq": jnp.zeros((64, 128), F32),
        }
        passes = (("top", wide_scores, None), ("sums", wide_sums, wide_out), ("dq", wide_grads, wide_rows))

        def scores(t):
            t["qd_t"] = qdt_ref[:, pl.ds(t["at"], tile)]
            rhs = spread(t["qd_t"])
            t["near"], t["far"] = mm(kv_ref[t["win"], :], rhs), mm(mkv, rhs)

        def softmax(t):
            s_near = jnp.where(
                usable(t["at"], 2 * tile, length), t["near"][:, 0:128] + tb_ref[...], NEG_BIG
            )
            s_far = t["far"][:, 0:128]
            high = jnp.maximum(
                jnp.max(s_near, axis=0, keepdims=True), jnp.max(s_far, axis=0, keepdims=True)
            )
            e_near, e_far = jnp.exp(s_near - high), jnp.exp(s_far - high)
            inv = keep_ref[:, pl.ds(t["at"], tile)] / (
                jnp.sum(e_near, axis=0, keepdims=True) + jnp.sum(e_far, axis=0, keepdims=True)
            )
            t["p_near"], t["p_far"] = e_near * inv, e_far * inv
            t["pb_near"], t["pb_far"] = t["p_near"].astype(BF16), t["p_far"].astype(BF16)

        def forward(t):
            out = mm(kvt_ref[64:128, t["win"]], t["pb_near"]) + mm(mkv_t[64:128], t["pb_far"])
            t["out"] = out.astype(BF16).astype(F32)

        def score_grads(t):
            row_dot = jnp.sum(t["qd_t"][64:128].astype(F32) * t["out"], axis=0, keepdims=True)
            ds_near = t["p_near"] * (t["near"][:, 128:256] - row_dot)
            ds_far = t["p_far"] * (t["far"][:, 128:256] - row_dot)
            t["bias"] += ds_near
            t["db_near"], t["db_far"] = ds_near.astype(BF16), ds_far.astype(BF16)

        def backward(t):
            back = stack(x_ref[t["slot"], :, 128:256] * scales)
            dq = mm(kvt_ref[0:64, t["win"]], t["db_near"]) + mm(mkv_t[0:64], t["db_far"])
            t["dq"] = dq * scale
            t["d_near"] = mm(side(t["db_near"], t["pb_near"]), back)
            t["d_far"] = mm(side(t["db_far"], t["pb_far"]), back)

        def write(t):
            d, o = t["dq"], t["out"]
            if t["first_half"]:
                placed = mm(wide["rows"], pick_ref[:, pl.ds(t["at"], tile)])
                o = o + placed[64:128]
                d = d + (placed[0:64] + placed[128:192])
            y_ref[t["slot"], tile : 2 * tile, :] = jnp.concatenate([d, o], axis=0).astype(BF16).T

        stages = (scores, softmax, forward, score_grads, backward, write)

        def band(first_half, between, i, c):
            tiles = []
            bias, tail, far = gb_ref[...], 0.0, gm_ref[...]
            for u in range(BAND_GROUP):
                slot = i * BAND_GROUP + u
                at = aligned(slot * tile, tile)
                half = slot < slots // 2 if first_half is None else first_half
                tiles.append({"slot": slot, "at": at, "win": pl.ds(at, 2 * tile), "first_half": half})
            for step in range(BAND_GROUP + SKEW * (len(stages) - 1)):
                for work in between.get(step, ()):
                    work()
                for k, stage in enumerate(stages):
                    u = step - SKEW * k
                    if not 0 <= u < BAND_GROUP:
                        continue
                    t = tiles[u]
                    if stage is score_grads:
                        t["bias"] = bias
                    stage(t)
                    if stage is score_grads:
                        bias = t["bias"]
                    if stage is backward:
                        ww_ref[pl.ds(t["at"], tile), 0:128] += tail + t["d_near"][0:tile]
                        tail = t["d_near"][tile:]
                        far = far + t["d_far"]
            ww_ref[pl.ds(aligned(tiles[-1]["at"] + tile, tile), tile), 0:128] += tail
            gb_ref[...] = bias
            gm_ref[...] = far
            return c

        rounds = slots // BAND_GROUP
        if rounds == 1:
            between = {}
            part = WIDE_TILES * tile
            cuts = list(range(0, frames, part))
            for k, (name, body, after) in enumerate(passes):
                for j, at in enumerate(cuts):

                    def work(name=name, body=body, at=at, last=j == len(cuts) - 1, after=after):
                        wide[name] = body(at, part + tile if last else part, wide[name])
                        if last and after is not None:
                            after()

                    step = WIDE_FIRST + k * WIDE_STEP + j * WIDE_STEP // len(cuts)
                    between.setdefault(step, []).append(work)
            band(None, between, 0, 0)
        else:
            for name, body, after in passes:
                wide[name] = over_rows(body, wide[name])
                if after is not None:
                    after()
            repeat(0, rounds // 2, functools.partial(band, True, {}), 0)
            repeat(rounds // 2, rounds, functools.partial(band, False, {}), 0)

        wide_bias = jnp.concatenate([gb_ref[...], jnp.zeros((128, 128), F32)], axis=0).T
        bias_sum = jnp.sum(shear(wide_bias, blk - 1, -1), axis=0, keepdims=True)[:, 0:256]
        b0 = bias_sum.astype(BF16).astype(F32)
        b1 = (bias_sum - b0).astype(BF16).astype(F32)
        b2 = bias_sum - b0 - b1
        bias_rows = [b[:, at : at + 128] for b in (b0, b1, b2) for at in (0, 128)]
        bias_rows = jnp.concatenate(bias_rows + [jnp.zeros((BIAS_ROWS - 6, 128), F32)], axis=0)
        bias_rows = bias_rows.astype(BF16)

        mem_back = jnp.concatenate(split2(gm_ref[...]), axis=0)

        def finish(first_half):
            def body(i, c):
                at = aligned(i * chunk, chunk)
                grads = ww_ref[pl.ds(aligned(at + blk, blk), chunk), 0:128]
                if first_half:
                    pick = (wide_row == wide_sub + at).astype(BF16)
                    grads = grads + mm(side(pick, pick), mem_back)
                y_ref[pl.ds(i * GROUP, GROUP), 0:tile, :] = grads.astype(BF16).reshape(
                    GROUP, tile, 128
                )
                for u in range(GROUP):
                    y_ref[i * GROUP + u, 2 * tile :, :] = bias_rows
                return c

            return body

        repeat(0, steps // 2, finish(True), 0)
        repeat(steps // 2, steps, finish(False), 0)


def vmem(shape, dtype):
    return pltpu.VMEM(shape, dtype)


def grant(frames):
    return pltpu.CompilerParams(vmem_limit_bytes=min(16 * frames // 2048, 60) * 1024 * 1024)


def core_call(by_head, rows, position_bias):
    slots, tile, _ = by_head.shape
    frames = slots * tile
    return pl.pallas_call(
        core_kernel,
        out_shape=jax.ShapeDtypeStruct((slots, 2 * tile + BIAS_ROWS, 128), BF16),
        scratch_shapes=[
            vmem((frames + tile, 128), BF16),
            vmem((128, frames + tile), BF16),
            vmem((128, frames), BF16),
            vmem((frames + tile, 256), F32),
            vmem((2 * tile, 128), F32),
            vmem((2 * tile, 128), F32),
            vmem((128, 128), F32),
            vmem((128, frames // 2), BF16),
            vmem((1, frames), F32),
        ],
        compiler_params=grant(frames),
    )(rows, position_bias, by_head)


def local(
    frame_queries, frame_keys, frame_values, cotangent, frame_mask, global_rows, position_bias
):
    slots = lax.axis_size("seq")
    tile, width = frame_queries.shape
    heads, span = position_bias.shape
    memory = global_rows.shape[0]
    frames = slots * tile

    hbm = pl.BlockSpec(memory_space=pltpu.MemorySpace.HBM)
    whole = pltpu.VMEM((tile, width), BF16)
    packed = pl.pallas_call(
        pack_kernel,
        out_shape=jax.ShapeDtypeStruct((slots, tile, 256), BF16),
        in_specs=[hbm] * 5,
        scratch_shapes=[
            pltpu.VMEM((1, tile), jnp.int32),
            whole,
            whole,
            whole,
            whole,
            pltpu.SemaphoreType.DMA((5,)),
        ],
        compiler_params=grant(frames),
    )(
        *(
            pltpu.with_memory_space_constraint(x, pltpu.MemorySpace.HBM)
            for x in (
                frame_mask.reshape(1, tile),
                frame_keys,
                frame_values,
                frame_queries,
                cotangent,
            )
        )
    )
    by_head = lax.all_to_all(packed, "seq", 0, 0, tiled=True)
    grads = core_call(by_head, global_rows.reshape(1, memory), position_bias)
    by_frame = lax.all_to_all(grads, "seq", 0, 0, tiled=True)
    rows = jax.ShapeDtypeStruct((tile, width), BF16)
    attended, dq, dk, dv, grad_bias = pl.pallas_call(
        unpack_kernel,
        out_shape=(rows, rows, rows, rows, jax.ShapeDtypeStruct((heads, span), F32)),
        compiler_params=grant(frames),
    )(by_frame)
    return (attended, dq, dk, dv, grad_bias)


def solution(mesh):
    return jax.shard_map(
        local,
        mesh=mesh,
        in_specs=(
            P(("groups", "seq"), None),
            P(("groups", "seq"), None),
            P(("groups", "seq"), None),
            P(("groups", "seq"), None),
            P(("groups", "seq")),
            P("groups"),
            P(),
        ),
        out_specs=(
            P(("groups", "seq"), None),
            P(("groups", "seq"), None),
            P(("groups", "seq"), None),
            P(("groups", "seq"), None),
            P("groups", None),
        ),
        check_vma=False,
    )
```

```python
import functools

import jax
import jax.numpy as jnp
from jax import lax
from jax.experimental import pallas as pl
from jax.experimental.pallas import tpu as pltpu
from jax.sharding import PartitionSpec as P

NEG_BIG = -1e30
DEAD = 64.0
BIAS_ROWS = 8
GROUP = 8
BAND_GROUP = 16
SKEW = 4
WIDE_FIRST = 0
WIDE_TILES = 2
WIDE_STEP = 5
BF16 = jnp.bfloat16
F32 = jnp.float32


def mm(a, b):
    return jnp.dot(a, b, preferred_element_type=F32)


def split2(x):
    high = x.astype(BF16)
    return high, (x - high.astype(F32)).astype(BF16)


def iota(shape, dim):
    return lax.broadcasted_iota(jnp.int32, shape, dim)


def swap_halves(x):
    half = x.shape[1] // 2
    return jnp.concatenate([x[:, half:], x[:, :half]], axis=1)


def pack_kernel(*refs):
    sources, out_ref, held, sem = refs[:5], refs[5], refs[6:11], refs[11]
    copies = [
        pltpu.make_async_copy(source, here, sem.at[i])
        for i, (source, here) in enumerate(zip(sources, held))
    ]
    for copy in copies:
        copy.start()
    mask_ref, k_ref, v_ref, q_ref, g_ref = held
    slots, rows, _ = out_ref.shape
    pairs = q_ref.shape[1] // 128
    low = iota((rows, 128), 1) < 64

    @pl.loop(2 * pairs, slots)
    def _(s):
        out_ref[s] = jnp.zeros(out_ref.shape[1:], BF16)

    for copy in copies[:3]:
        copy.wait()
    for i in range(pairs):
        at = slice(128 * i, 128 * (i + 1))
        even, odd = 2 * i, 2 * i + 1
        k, v = k_ref[:, at], v_ref[:, at]
        out_ref[even, :, 0:128] = jnp.where(low, k, swap_halves(v))
        out_ref[odd, :, 0:128] = jnp.where(low, swap_halves(k), v)
    for copy in copies[3:]:
        copy.wait()
    alive = iota((rows, 128), 0) < jnp.sum(mask_ref[...])
    for i in range(pairs):
        at = slice(128 * i, 128 * (i + 1))
        q, g = q_ref[:, at], jnp.where(alive, g_ref[:, at], jnp.asarray(DEAD, BF16))
        even, odd = 2 * i, 2 * i + 1
        out_ref[even, :, 128:256] = jnp.where(low, q, swap_halves(g))
        out_ref[odd, :, 128:256] = jnp.where(low, swap_halves(q), g)


def unpack_kernel(in_ref, att_ref, dq_ref, dk_ref, dv_ref, gb_ref):
    rows = att_ref.shape[0]
    pairs = att_ref.shape[1] // 128
    low = iota((rows, 128), 1) < 64
    for i in range(pairs):
        at = slice(128 * i, 128 * (i + 1))
        even, odd = 2 * i, 2 * i + 1
        a, b = in_ref[even, :rows, :], in_ref[odd, :rows, :]
        dk_ref[:, at] = jnp.where(low, a, swap_halves(b))
        dv_ref[:, at] = jnp.where(low, swap_halves(a), b)
        a, b = in_ref[even, rows : 2 * rows, :], in_ref[odd, rows : 2 * rows, :]
        dq_ref[:, at] = jnp.where(low, a, swap_halves(b))
        att_ref[:, at] = jnp.where(low, swap_halves(a), b)
    for h in range(2 * pairs):
        parts = in_ref[h, 2 * rows :, :].astype(F32)
        whole = parts[0:2] + parts[2:4] + parts[4:6]
        whole = jnp.concatenate([whole[0:1], whole[1:2]], axis=1)
        gb_ref[h : h + 1, :] = whole[:, : gb_ref.shape[1]]


def repeat(first, last, body, carry):
    if last - first > 2:
        return lax.fori_loop(first, last, body, carry)
    for i in range(first, last):
        carry = body(i, carry)
    return carry


def aligned(x, size):
    return x if isinstance(x, int) else pl.multiple_of(x, size)


def shear(x, first, step):
    rows, lanes = x.shape
    row = iota(x.shape, 0)
    x = pltpu.roll(x, first % lanes, 1)
    bit = 1
    while bit < rows:
        x = jnp.where((row & bit) != 0, pltpu.roll(x, (step * bit) % lanes, 1), x)
        bit *= 2
    return x


def core_kernel(
    rows_ref, bias_ref, x_ref, y_ref, kv_ref, kvt_ref, qdt_ref, ww_ref, tb_ref, gb_ref, gm_ref, pick_ref, keep_ref
):
    slots, tile, _ = x_ref.shape
    frames = slots * tile
    blk = tile // 2
    heads, span = bias_ref.shape
    memory = rows_ref.shape[1]
    scale = 64 ** (-0.5)
    owner = lax.axis_index("seq")
    chunk = GROUP * tile
    steps = slots // GROUP

    @pl.when(owner < heads)
    def _():
        lane = iota((128, 128), 1)
        sub = iota((128, 128), 0)
        low_lane = lane < 64
        low_row = sub < 64
        gr_row = jnp.broadcast_to(rows_ref[...], (128, memory))
        gr_col = gr_row.T
        zero_t = jnp.zeros((128, 128), BF16)

        def side(top, bottom):
            return jnp.concatenate([top, bottom], axis=1)

        def spread(x_t):
            return side(jnp.where(low_row, x_t, zero_t), jnp.where(low_row, zero_t, x_t))

        def stack(x):
            return jnp.concatenate(
                [jnp.where(low_lane, x, zero_t), jnp.where(low_lane, zero_t, x)], axis=0
            )

        def over_rows(body, carry):
            carry = repeat(
                0, steps - 1, lambda i, c: body(aligned(i * chunk, chunk), chunk, c), carry
            )
            return body(frames - chunk, chunk + tile, carry)

        def usable(at, rows, length):
            place = iota((rows, 128), 0) + (at - blk)
            inside = place < length
            if isinstance(at, int) and at >= blk:
                if at + rows - blk <= frames // 2:
                    return None
                return inside
            return (place >= 0) & inside

        zeros = jnp.zeros((blk, 128), BF16)
        kv_ref[0:blk, :] = zeros
        kv_ref[frames + blk :, :] = zeros
        wide_sub = iota((chunk, 128), 0)
        wide_lane = iota((128, chunk), 1)
        wide_row = jnp.broadcast_to(gr_row[0:1], (chunk, memory))
        wide_col = jnp.concatenate([gr_col] * GROUP, axis=1)
        ones = jnp.ones((16, memory), BF16)
        scales = jnp.where(iota((1, 128), 1) < 64, scale, 1.0).astype(BF16)

        def prepare(first_half):
            def body(i, c):
                count, mem = c
                at = aligned(i * chunk, chunk)
                x = x_ref[pl.ds(i * GROUP, GROUP)].reshape(chunk, 256)
                kv_ref[pl.ds(aligned(at + blk, blk), chunk), :] = x[:, 0:128]
                qd_t = (x[:, 128:256] * scales).T
                qdt_ref[:, pl.ds(at, chunk)] = qd_t
                alive = (qd_t[64:80].astype(F32)[0:1] < 0.5 * DEAD).astype(F32)
                if first_half:
                    pick = (wide_col == wide_lane + at).astype(BF16)
                    pick_ref[:, pl.ds(at, chunk)] = pick
                    mem = mem + mm(pick, x)
                    keep_ref[:, pl.ds(at, chunk)] = alive - mm(ones, pick)[0:1]
                else:
                    keep_ref[:, pl.ds(at, chunk)] = alive
                return count + jnp.sum(alive, axis=1, keepdims=True), mem

            return body

        carry = (jnp.zeros((1, 1), F32), jnp.zeros((128, 256), F32))
        carry = repeat(0, steps // 2, prepare(True), carry)
        count, mem = repeat(steps // 2, steps, prepare(False), carry)
        length = count.astype(jnp.int32)
        mkv = mem[:, 0:128].astype(BF16)
        mqo = jnp.where(low_lane, mem[:, 128:256] * scale, mem[:, 128:256]).astype(BF16)
        mkv_t = mkv.T
        mqo_t = mqo.T

        head = jnp.minimum(owner, heads - 1)
        b_row = side(bias_ref[pl.ds(head, 1), :], jnp.zeros((1, 384 - span), F32))
        table = shear(jnp.broadcast_to(b_row, (128, 384)), 1 - blk, 1)[:, : 2 * tile].T
        gap = iota(table.shape, 0) // blk - iota(table.shape, 1) // blk
        tb_ref[...] = jnp.where((gap >= 0) & (gap <= 2), table, NEG_BIG)
        gb_ref[...] = jnp.zeros_like(gb_ref)
        gm_ref[...] = jnp.zeros_like(gm_ref)

        wide_rhs = spread(mqo_t)
        wide_back = stack(mqo)

        def wide_scores(at, rows, top):
            kv = kv_ref[pl.ds(at, rows), :]
            kvt_ref[:, pl.ds(at, rows)] = kv.T
            both = mm(kv, wide_rhs)
            w = both[:, 0:128]
            can = usable(at, rows, length)
            if can is not None:
                w = jnp.where(can, w, NEG_BIG)
            ww_ref[pl.ds(at, rows), 0:128] = w
            ww_ref[pl.ds(at, rows), 128:256] = both[:, 128:256]
            return jnp.maximum(top, jnp.max(w, axis=0, keepdims=True))

        def wide_sums(at, rows, c):
            total, numer = c
            e = jnp.exp(ww_ref[pl.ds(at, rows), 0:128] - wide["top"])
            ww_ref[pl.ds(at, rows), 0:128] = e
            high, rest = split2(e)
            numer = numer + mm(kvt_ref[64:128, pl.ds(at, rows)], side(high, rest))
            return total + jnp.sum(e, axis=0, keepdims=True), numer

        def wide_out():
            total, numer = wide["sums"]
            mem_out = ((numer[:, 0:128] + numer[:, 128:256]) / total).astype(BF16)
            wide["out"] = mem_out
            wide["dot"] = jnp.sum(
                mqo_t[64:128].astype(F32) * mem_out.astype(F32), axis=0, keepdims=True
            )
            wide["share"] = 1.0 / total

        def wide_grads(at, rows, dq):
            p = ww_ref[pl.ds(at, rows), 0:128] * wide["share"]
            dw = (p * (ww_ref[pl.ds(at, rows), 128:256] - wide["dot"])).astype(BF16)
            ww_ref[pl.ds(at, rows), 0:128] = mm(side(dw, p.astype(BF16)), wide_back)
            return dq + mm(kvt_ref[0:64, pl.ds(at, rows)], dw)

        def wide_rows():
            high, rest = split2(wide["dq"] * scale)
            wide["rows"] = jnp.concatenate([high, wide["out"], rest], axis=0)

        wide = {
            "top": jnp.full((1, 128), NEG_BIG, F32),
            "sums": (jnp.zeros((1, 128), F32), jnp.zeros((64, 256), F32)),
            "dq": jnp.zeros((64, 128), F32),
        }
        passes = (("top", wide_scores, None), ("sums", wide_sums, wide_out), ("dq", wide_grads, wide_rows))

        def scores(t):
            t["qd_t"] = qdt_ref[:, pl.ds(t["at"], tile)]
            rhs = spread(t["qd_t"])
            t["near"], t["far"] = mm(kv_ref[t["win"], :], rhs), mm(mkv, rhs)

        def softmax(t):
            s_near = t["near"][:, 0:128] + tb_ref[...]
            can = usable(t["at"], 2 * tile, length)
            if can is not None:
                s_near = jnp.where(can, s_near, NEG_BIG)
            s_far = t["far"][:, 0:128]
            high = jnp.maximum(
                jnp.max(s_near, axis=0, keepdims=True), jnp.max(s_far, axis=0, keepdims=True)
            )
            e_near, e_far = jnp.exp(s_near - high), jnp.exp(s_far - high)
            inv = keep_ref[:, pl.ds(t["at"], tile)] / (
                jnp.sum(e_near, axis=0, keepdims=True) + jnp.sum(e_far, axis=0, keepdims=True)
            )
            t["p_near"], t["p_far"] = e_near * inv, e_far * inv
            t["pb_near"], t["pb_far"] = t["p_near"].astype(BF16), t["p_far"].astype(BF16)

        def forward(t):
            out = mm(kvt_ref[64:128, t["win"]], t["pb_near"]) + mm(mkv_t[64:128], t["pb_far"])
            t["out"] = out.astype(BF16).astype(F32)

        def score_grads(t):
            row_dot = jnp.sum(t["qd_t"][64:128].astype(F32) * t["out"], axis=0, keepdims=True)
            ds_near = t["p_near"] * (t["near"][:, 128:256] - row_dot)
            ds_far = t["p_far"] * (t["far"][:, 128:256] - row_dot)
            t["bias"] += ds_near
            t["db_near"], t["db_far"] = ds_near.astype(BF16), ds_far.astype(BF16)

        def backward(t):
            back = stack(x_ref[t["slot"], :, 128:256] * scales)
            dq = mm(kvt_ref[0:64, t["win"]], t["db_near"]) + mm(mkv_t[0:64], t["db_far"])
            t["dq"] = dq * scale
            t["d_near"] = mm(side(t["db_near"], t["pb_near"]), back)
            t["d_far"] = mm(side(t["db_far"], t["pb_far"]), back)

        def write(t):
            d, o = t["dq"], t["out"]
            if t["first_half"]:
                placed = mm(wide["rows"], pick_ref[:, pl.ds(t["at"], tile)])
                o = o + placed[64:128]
                d = d + (placed[0:64] + placed[128:192])
            y_ref[t["slot"], tile : 2 * tile, :] = jnp.concatenate([d, o], axis=0).astype(BF16).T

        stages = (scores, softmax, forward, score_grads, backward, write)

        def settle(slot):
            y_ref[slot, 0:tile, :] = ww_ref[pl.ds(slot * tile + blk, tile), 0:128].astype(BF16)

        def band(first_half, between, i, c):
            tiles = []
            bias, tail, far = gb_ref[...], 0.0, gm_ref[...]
            for u in range(BAND_GROUP):
                slot = i * BAND_GROUP + u
                at = aligned(slot * tile, tile)
                half = slot < slots // 2 if first_half is None else first_half
                tiles.append({"slot": slot, "at": at, "win": pl.ds(at, 2 * tile), "first_half": half})
            for step in range(BAND_GROUP + SKEW * (len(stages) - 1)):
                for work in between.get(step, ()):
                    work()
                for k, stage in enumerate(stages):
                    u = step - SKEW * k
                    if not 0 <= u < BAND_GROUP:
                        continue
                    t = tiles[u]
                    if stage is score_grads:
                        t["bias"] = bias
                    stage(t)
                    if stage is score_grads:
                        bias = t["bias"]
                    if stage is backward:
                        ww_ref[pl.ds(t["at"], tile), 0:128] += tail + t["d_near"][0:tile]
                        tail = t["d_near"][tile:]
                        far = far + t["d_far"]
                        if first_half is None and t["slot"] > slots // 2:
                            settle(t["slot"] - 1)
            ww_ref[pl.ds(aligned(tiles[-1]["at"] + tile, tile), tile), 0:128] += tail
            if first_half is None:
                settle(tiles[-1]["slot"])
            gb_ref[...] = bias
            gm_ref[...] = far
            return c

        rounds = slots // BAND_GROUP
        if rounds == 1:
            between = {}
            part = WIDE_TILES * tile
            cuts = list(range(0, frames, part))
            for k, (name, body, after) in enumerate(passes):
                for j, at in enumerate(cuts):

                    def work(name=name, body=body, at=at, last=j == len(cuts) - 1, after=after):
                        wide[name] = body(at, part + tile if last else part, wide[name])
                        if last and after is not None:
                            after()

                    step = WIDE_FIRST + k * WIDE_STEP + j * WIDE_STEP // len(cuts)
                    between.setdefault(step, []).append(work)
            band(None, between, 0, 0)
        else:
            for name, body, after in passes:
                wide[name] = over_rows(body, wide[name])
                if after is not None:
                    after()
            repeat(0, rounds // 2, functools.partial(band, True, {}), 0)
            repeat(rounds // 2, rounds, functools.partial(band, False, {}), 0)

        wide_bias = jnp.concatenate([gb_ref[...], jnp.zeros((128, 128), F32)], axis=0).T
        bias_sum = jnp.sum(shear(wide_bias, blk - 1, -1), axis=0, keepdims=True)[:, 0:256]
        b0 = bias_sum.astype(BF16).astype(F32)
        b1 = (bias_sum - b0).astype(BF16).astype(F32)
        b2 = bias_sum - b0 - b1
        bias_rows = [b[:, at : at + 128] for b in (b0, b1, b2) for at in (0, 128)]
        bias_rows = jnp.concatenate(bias_rows + [jnp.zeros((BIAS_ROWS - 6, 128), F32)], axis=0)
        bias_rows = bias_rows.astype(BF16)

        mem_back = jnp.concatenate(split2(gm_ref[...]), axis=0)

        def finish(first_half):
            def body(i, c):
                at = aligned(i * chunk, chunk)
                grads = ww_ref[pl.ds(aligned(at + blk, blk), chunk), 0:128]
                if first_half:
                    pick = (wide_row == wide_sub + at).astype(BF16)
                    grads = grads + mm(side(pick, pick), mem_back)
                y_ref[pl.ds(i * GROUP, GROUP), 0:tile, :] = grads.astype(BF16).reshape(
                    GROUP, tile, 128
                )
                return c

            return body

        repeat(0, steps // 2, finish(True), 0)
        if rounds > 1:
            repeat(steps // 2, steps, finish(False), 0)

        @pl.loop(0, slots, unroll=slots <= 16)
        def _(slot):
            y_ref[slot, 2 * tile :, :] = bias_rows


def vmem(shape, dtype):
    return pltpu.VMEM(shape, dtype)


def grant(frames):
    return pltpu.CompilerParams(vmem_limit_bytes=min(16 * frames // 2048, 60) * 1024 * 1024)


def core_call(by_head, rows, position_bias):
    slots, tile, _ = by_head.shape
    frames = slots * tile
    return pl.pallas_call(
        core_kernel,
        out_shape=jax.ShapeDtypeStruct((slots, 2 * tile + BIAS_ROWS, 128), BF16),
        scratch_shapes=[
            vmem((frames + tile, 128), BF16),
            vmem((128, frames + tile), BF16),
            vmem((128, frames), BF16),
            vmem((frames + tile, 256), F32),
            vmem((2 * tile, 128), F32),
            vmem((2 * tile, 128), F32),
            vmem((128, 128), F32),
            vmem((128, frames // 2), BF16),
            vmem((1, frames), F32),
        ],
        compiler_params=grant(frames),
    )(rows, position_bias, by_head)


def local(
    frame_queries, frame_keys, frame_values, cotangent, frame_mask, global_rows, position_bias
):
    slots = lax.axis_size("seq")
    tile, width = frame_queries.shape
    heads, span = position_bias.shape
    memory = global_rows.shape[0]
    frames = slots * tile

    hbm = pl.BlockSpec(memory_space=pltpu.MemorySpace.HBM)
    whole = pltpu.VMEM((tile, width), BF16)
    packed = pl.pallas_call(
        pack_kernel,
        out_shape=jax.ShapeDtypeStruct((slots, tile, 256), BF16),
        in_specs=[hbm] * 5,
        scratch_shapes=[
            pltpu.VMEM((1, tile), jnp.int32),
            whole,
            whole,
            whole,
            whole,
            pltpu.SemaphoreType.DMA((5,)),
        ],
        compiler_params=grant(frames),
    )(
        *(
            pltpu.with_memory_space_constraint(x, pltpu.MemorySpace.HBM)
            for x in (
                frame_mask.reshape(1, tile),
                frame_keys,
                frame_values,
                frame_queries,
                cotangent,
            )
        )
    )
    by_head = lax.all_to_all(packed, "seq", 0, 0, tiled=True)
    grads = core_call(by_head, global_rows.reshape(1, memory), position_bias)
    by_frame = lax.all_to_all(grads, "seq", 0, 0, tiled=True)
    rows = jax.ShapeDtypeStruct((tile, width), BF16)
    attended, dq, dk, dv, grad_bias = pl.pallas_call(
        unpack_kernel,
        out_shape=(rows, rows, rows, rows, jax.ShapeDtypeStruct((heads, span), F32)),
        compiler_params=grant(frames),
    )(by_frame)
    return (attended, dq, dk, dv, grad_bias)


def solution(mesh):
    return jax.shard_map(
        local,
        mesh=mesh,
        in_specs=(
            P(("groups", "seq"), None),
            P(("groups", "seq"), None),
            P(("groups", "seq"), None),
            P(("groups", "seq"), None),
            P(("groups", "seq")),
            P("groups"),
            P(),
        ),
        out_specs=(
            P(("groups", "seq"), None),
            P(("groups", "seq"), None),
            P(("groups", "seq"), None),
            P(("groups", "seq"), None),
            P("groups", None),
        ),
        check_vma=False,
    )
```
